512 devices in a mesh: row: 32 (over z_lo, y), col: 16 (over x, z_hi, core).
Axes of the slice: x: 4, y: 4, z: 16 (z_hi: 2, z_lo: 8; z = z_hi * 8 + z_lo), core: 2. Of those that a mesh axis runs over, the one named last changes fastest.
Arguments:
- pair_slab: bfloat16 [64, 1024, 128], P('col', 'row'), may hold values from -6 to 6
- pair_full: bfloat16 [1024, 1024, 128], P('col', 'row'), may hold values from -6 to 6
- grad_out: bfloat16 [64, 1024, 128], P('row', 'col'), may hold values from -0.59765625 to 0.59765625
- w_a_lin: bfloat16 [128, 128], replicated, may hold values from -0.5 to 0.5
- w_a_gate: bfloat16 [128, 128], replicated, may hold values from -0.5 to 0.5
- w_b_lin: bfloat16 [128, 128], replicated, may hold values from -0.5 to 0.5
- w_b_gate: bfloat16 [128, 128], replicated, may hold values from -0.5 to 0.5
- mask_slab: int32 [64], replicated, may hold values 0 or 1
- mask_residue: int32 [1024], replicated, may hold values 0 or 1
Outputs:
- grad_slab: bfloat16 [64, 1024, 128], P('col', 'row')
- grad_pair: bfloat16 [1024, 1024, 128], P('col', 'row')
- grad_weights: float32 [4, 128, 128], replicated
The draws below stay inside these ranges and needn't reach their ends.
All inputs are finite; a program needn't handle non-finite values.
Results may differ from the reference program's by a relative error of at most 0.0057.
Values may be sent and summed in bfloat16 or wider, within the bound.
A program may use at most 64 MiB of HBM per device.

```python
import jax
import jax.numpy as jnp
from jax import lax

CZ = 128
CH = 128
N = 1024
I = 64
N_COL = 16


def set_ends(values, stream_key, smallest, high):
    longest = values.shape.index(max(values.shape))
    spots = []
    for shift in (0, 1):
        where = [jax.random.randint(jax.random.fold_in(stream_key, axis), (), 0, length) for axis, length in enumerate(values.shape)]
        where[longest] = (where[longest] + shift) % values.shape[longest]
        spots.append(tuple(where))
    return values.at[spots[0]].set(smallest).at[spots[1]].set(high)


def levels(key, shape, shards, smallest, top_value):
    factor_of, own = 1.0, jax.random.fold_in(key, 6)
    for dim, parts in shards:
        heights = jnp.exp(jax.random.uniform(jax.random.fold_in(own, dim), (parts,), jnp.float32, smallest / len(shards), top_value / len(shards)))
        factor_of = factor_of * jnp.repeat(heights, shape[dim] // parts).reshape([-1 if axis == dim else 1 for axis in range(len(shape))])
    return factor_of


def bell_draw(own_key, dims, deviation, most, cuts=(), dtype=jnp.bfloat16):
    entries = deviation * jax.random.normal(own_key, dims, jnp.float32)
    if cuts:
        entries = entries * levels(own_key, dims, cuts, -0.22, 0.18)
    return jnp.clip(entries, -most, most).astype(dtype)


def setup_inputs(seed: int = 0) -> dict:
    streams_of = jax.random.split(jax.random.key(seed), 10)
    return {
        "pair_slab": bell_draw(streams_of[0], (I, N, CZ), 1.0, 6.0, ((0, 16), (1, 32))),
        "pair_full": bell_draw(streams_of[1], (N, N, CZ), 1.0, 6.0, ((0, 16), (1, 32))),
        "grad_out": bell_draw(streams_of[2], (I, N, CH), 0.1, 0.59765625, ((0, 32), (1, 16))),
        "w_a_lin": bell_draw(streams_of[3], (CZ, CH), CZ ** -0.5, 0.5),
        "w_a_gate": bell_draw(streams_of[4], (CZ, CH), CZ ** -0.5, 0.5),
        "w_b_lin": bell_draw(streams_of[5], (CZ, CH), CZ ** -0.5, 0.5),
        "w_b_gate": bell_draw(streams_of[6], (CZ, CH), CZ ** -0.5, 0.5),
        "mask_slab": set_ends((jax.random.randint(streams_of[7], (I,), 0, 8) < 7).astype(jnp.int32), jax.random.fold_in(streams_of[7], 1), 0, 1),
        "mask_residue": set_ends((jax.random.randint(streams_of[8], (N,), 0, 8) < 7).astype(jnp.int32), jax.random.fold_in(streams_of[8], 1), 0, 1),
    }


def narrow(values):
    return lax.optimization_barrier(values.astype(jnp.bfloat16)).astype(jnp.float32)


def project(pair, weight):
    return jnp.einsum('rkd,dc->rkc', pair.astype(jnp.float32), weight.astype(jnp.float32))


def forward_gate(pair, w_linear, w_gate, mask):
    linear = project(pair, w_linear)
    sigmoid = jax.nn.sigmoid(project(pair, w_gate))
    value = narrow(mask * sigmoid * linear)
    return linear, sigmoid, value


def gate_back(grad, mask, linear, sigmoid):
    d_linear = narrow(grad * mask * sigmoid)
    d_gate = narrow(grad * mask * linear * sigmoid * (1.0 - sigmoid))
    return d_linear, d_gate


def input_grads(pair, d_linear, d_gate, w_linear, w_gate):
    pair_wide = pair.astype(jnp.float32)
    input_grad = jnp.einsum('rkc,dc->rkd', d_linear, w_linear.astype(jnp.float32))
    input_grad = input_grad + jnp.einsum('rkc,dc->rkd', d_gate, w_gate.astype(jnp.float32))
    weight_linear = jnp.einsum('rkd,rkc->dc', pair_wide, d_linear)
    weight_gate = jnp.einsum('rkd,rkc->dc', pair_wide, d_gate)
    return input_grad.astype(jnp.bfloat16), weight_linear, weight_gate


def reference(pair_slab, pair_full, grad_out, w_a_lin, w_a_gate, w_b_lin, w_b_gate, mask_slab, mask_residue):
    slab_flags = mask_slab.astype(jnp.float32)
    res_flags = mask_residue.astype(jnp.float32)
    slab_mask = (slab_flags[:, None] * res_flags[None, :])[:, :, None]
    slab_linear, slab_sigmoid, slab_value = forward_gate(pair_slab, w_a_lin, w_a_gate, slab_mask)
    block_width = N // N_COL
    pair_blocks = pair_full.reshape(N_COL, block_width, N, CZ)
    grad_blocks = jnp.transpose(grad_out.reshape(I, N_COL, block_width, CH), (1, 0, 2, 3))
    flag_blocks = res_flags.reshape(N_COL, block_width)

    def visit_block(running, block_items):
        slab_sum, lin_sum, gate_sum = running
        pair_block, grad_block, flag_block = block_items
        pair_mask = (flag_block[:, None] * res_flags[None, :])[:, :, None]
        pair_linear, pair_sigmoid, pair_value = forward_gate(pair_block, w_b_lin, w_b_gate, pair_mask)
        grad_wide = grad_block.astype(jnp.float32)
        slab_sum = slab_sum + jnp.einsum('ijc,jkc->ikc', grad_wide, pair_value)
        pair_grad = jnp.einsum('ijc,ikc->jkc', grad_wide, slab_value)
        d_linear, d_gate = gate_back(pair_grad, pair_mask, pair_linear, pair_sigmoid)
        block_out, weight_linear, weight_gate = input_grads(pair_block, d_linear, d_gate, w_b_lin, w_b_gate)
        return (slab_sum, lin_sum + weight_linear, gate_sum + weight_gate), block_out

    start = (jnp.zeros((I, N, CH), jnp.float32), jnp.zeros((CZ, CH), jnp.float32), jnp.zeros((CZ, CH), jnp.float32))
    (slab_grad, pair_lin_w, pair_gate_w), pair_out = lax.scan(visit_block, start, (pair_blocks, grad_blocks, flag_blocks))
    grad_pair = pair_out.reshape(N, N, CZ)
    d_linear, d_gate = gate_back(slab_grad, slab_mask, slab_linear, slab_sigmoid)
    grad_slab, slab_lin_w, slab_gate_w = input_grads(pair_slab, d_linear, d_gate, w_a_lin, w_a_gate)
    grad_weights = jnp.stack([slab_lin_w, slab_gate_w, pair_lin_w, pair_gate_w]) / N
    return grad_slab, grad_pair, grad_weights
```

```python
import functools

import jax
import jax.numpy as jnp
from jax import lax
from jax.experimental import pallas as pl
from jax.experimental.pallas import tpu as pltpu
from jax.sharding import PartitionSpec as P

MESH = pl.DeviceIdType.MESH
F32 = jnp.float32
BF16 = jnp.bfloat16
VMEM = pl.BlockSpec(memory_space=pltpu.VMEM)
SMEM = pl.BlockSpec(memory_space=pltpu.SMEM)


class Here:
    def __init__(self):
        row = lax.axis_index("row")
        col = lax.axis_index("col")
        self.row, self.col = row, col
        self.z, self.y = row // 4, row % 4
        self.x, self.h, self.core = col // 4, (col // 2) % 2, col % 2

    def at(self, z=None, y=None, x=None, h=None, core=None):
        z = self.z if z is None else z
        y = self.y if y is None else y
        x = self.x if x is None else x
        h = self.h if h is None else h
        core = self.core if core is None else core
        return (z * 4 + y, x * 4 + h * 2 + core)


class Sender:
    def __init__(self, send_sems):
        self.send_sems = send_sems
        self.started = []

    def send(self, src, dst, recv_sem, device):
        copy = pltpu.make_async_remote_copy(
            src_ref=src,
            dst_ref=dst,
            send_sem=self.send_sems.at[len(self.started)],
            recv_sem=recv_sem,
            device_id=device,
            device_id_type=MESH,
        )
        copy.start()
        self.started.append(copy)

    def recv(self, dst, recv_sem, device):
        pltpu.make_async_remote_copy(
            src_ref=dst,
            dst_ref=dst,
            send_sem=self.send_sems.at[0],
            recv_sem=recv_sem,
            device_id=device,
            device_id_type=MESH,
        ).wait_recv()

    def finish(self):
        for copy in self.started:
            copy.wait_send()


def greet(peers):
    barrier = pltpu.get_barrier_semaphore()
    for peer in peers:
        pl.semaphore_signal(barrier, inc=1, device_id=peer, device_id_type=MESH)
    return lambda: pl.semaphore_wait(barrier, len(peers))


GATHER_SENDS = 7 + 32 + 15


def gather_kernel(grad_ref, slab_ref, grad_all, slab_all, send_sems, gz, gy, sh, sx, sc):
    me = Here()
    zg, zl = me.z // 4, me.z % 4
    group = [me.at(z=zg * 4 + (zl + d) % 4) for d in (1, 2, 3)]
    across = me.at(z=(1 - zg) * 4 + zl)
    up, down = me.at(y=(me.y + 1) % 4), me.at(y=(me.y + 3) % 4)
    far = me.at(h=1 - me.h)
    ring = [me.at(x=(me.x + d) % 4) for d in (1, 2, 3)]
    twin = me.at(core=1 - me.core)
    ready = greet(group + [across, up, down, far] + ring + [twin])
    ready()
    out = Sender(send_sems)

    def z_of(t):
        side = zg if t < 4 else 1 - zg
        return side * 4 + (zl + 4 - t % 4) % 4

    def block(t, y=None):
        return grad_all.at[z_of(t) * 4 + (me.y if y is None else y)]

    def col_of(u, d, core=None):
        h = me.h if u == 0 else 1 - me.h
        return ((me.x + 4 - d) % 4) * 4 + h * 2 + (me.core if core is None else core)

    own = grad_all.at[me.row]
    slab_own = slab_all.at[me.col]
    out.send(slab_ref, slab_own, sh.at[0], far)
    out.send(grad_ref, own, gz.at[3], across)
    for d in (1, 3, 2):
        out.send(grad_ref, own, gz.at[d - 1], group[d - 1])
    for side, peer in ((0, up), (1, down)):
        out.send(grad_ref, own, gy.at[0, side], peer)
    for d in (1, 3, 2):
        out.send(slab_ref, slab_own, sx.at[0, d - 1], ring[d - 1])
    out.send(slab_ref, slab_own, sc.at[0, 0], twin)
    grad_all[me.row] = grad_ref[...]
    slab_all[me.col] = slab_ref[...]

    below, above, across_y = (me.y + 3) % 4, (me.y + 1) % 4, (me.y + 2) % 4

    def relay(t):
        out.recv(block(t, below), gy.at[t, 0], down)
        half = block(t, below).at[0]
        out.send(half, half, gy.at[t, 2], up)
        out.recv(block(t, above), gy.at[t, 1], up)
        half = block(t, above).at[1]
        out.send(half, half, gy.at[t, 3], down)

    def slab_round(u):
        for d in (1, 3, 2):
            spot = slab_all.at[col_of(u, d)]
            out.recv(spot, sx.at[u, d - 1], ring[0])
            out.send(spot, spot, sc.at[u, d], twin)

    order = (0, 1, 3, 2, 4, 5, 7, 6)
    for n, t in enumerate(order):
        if t > 0:
            out.recv(block(t), gz.at[t - 1], across)
            if t == 4:
                for d in (1, 3, 2):
                    out.send(block(t), block(t), gz.at[3 + d], group[d - 1])
            out.send(block(t), block(t), gy.at[t, 0], up)
            out.send(block(t), block(t), gy.at[t, 1], down)
            relay(order[n - 1])
        if n == 2:
            slab_round(0)
        if n == 5:
            spot = slab_all.at[col_of(1, 0)]
            out.recv(spot, sh.at[0], far)
            for d in (1, 3, 2):
                out.send(spot, spot, sx.at[1, d - 1], ring[d - 1])
            out.send(spot, spot, sc.at[1, 0], twin)
    relay(order[-1])
    slab_round(1)
    for t in range(8):
        out.recv(block(t, across_y).at[0], gy.at[t, 2], down)
        out.recv(block(t, across_y).at[1], gy.at[t, 3], up)
    for u in range(2):
        for d in range(4):
            spot = slab_all.at[col_of(u, d, 1 - me.core)]
            out.recv(spot, sc.at[u, d], twin)
    out.finish()


def gather(grad_out, pair_slab):
    grad_all, slab_all = pl.pallas_call(
        gather_kernel,
        out_shape=(
            jax.ShapeDtypeStruct((32, 2, 64, 128), BF16),
            jax.ShapeDtypeStruct((16, 4, 32, 128), BF16),
        ),
        in_specs=[VMEM, VMEM],
        out_specs=(VMEM, VMEM),
        scratch_shapes=[
            pltpu.SemaphoreType.DMA((GATHER_SENDS,)),
            pltpu.SemaphoreType.DMA((7,)),
            pltpu.SemaphoreType.DMA((8, 4)),
            pltpu.SemaphoreType.DMA((1,)),
            pltpu.SemaphoreType.DMA((2, 3)),
            pltpu.SemaphoreType.DMA((2, 4)),
        ],
        compiler_params=pltpu.CompilerParams(collective_id=0, has_side_effects=True),
        name="gather",
    )(grad_out, pair_slab)
    return grad_all.reshape(4096, 128), slab_all.reshape(2048, 128)


def key_mask(mask_ref, base):
    spots = lax.broadcasted_iota(jnp.int32, (32, 128), 0)
    flags = jnp.zeros((32, 128), F32)
    for k in range(32):
        flags = jnp.where(spots == k, mask_ref[base + k].astype(F32), flags)
    return flags


def gates(rows, both, flags):
    product = jnp.dot(rows, both, preferred_element_type=F32)
    linear, sigmoid = product[:, :128], jax.nn.sigmoid(product[:, 128:])
    to_linear = flags * sigmoid
    return to_linear * linear, to_linear, to_linear * linear * (1.0 - sigmoid)


def local_kernel(
    grad_ref, slab_ref, pair_ref, wal, wag, wbl, wbg, mask_slab, mask_res,
    grad_pair, partial, weights,
    wide, both_a, both_b, slab_value, slab_lin, slab_gate, pair_value, pair_lin, pair_gate, both_d,
):
    row, col = lax.axis_index("row"), lax.axis_index("col")
    both_a[:, :128], both_a[:, 128:] = wal[...], wag[...]
    both_b[:, :128], both_b[:, 128:] = wbl[...], wbg[...]
    keys = key_mask(mask_res, row * 32)

    def forward(n, first, mask, source, both, value, to_lin, to_gate):
        rows = pl.ds(pl.multiple_of(n * 256, 256), 256)
        flags = jnp.concatenate(
            [keys * mask[first + n * 8 + m].astype(F32) for m in range(8)], axis=0
        )
        val, lin, gate = gates(source[rows, :], both[...], flags)
        value[rows, :] = val.astype(BF16).astype(F32)
        to_lin[rows, :] = lin
        to_gate[rows, :] = gate

    @pl.loop(0, 8)
    def _(n):
        forward(n, 0, mask_slab, slab_ref, both_a, slab_value, slab_lin, slab_gate)
        forward(n, col * 64, mask_res, pair_ref, both_b, pair_value, pair_lin, pair_gate)
        rows = pl.ds(pl.multiple_of(n * 512, 512), 512)
        wide[rows, :] = grad_ref[rows, :].astype(F32)

    def contract(scalar_row, vectors):
        def step(s, acc):
            lanes = [vectors[pl.ds(pl.multiple_of(s * 32 + t * 8, 8), 8), :] for t in range(4)]
            new = []
            for m in range(8):
                factor = wide[pl.ds(scalar_row(s, m), 8, stride=0), :]
                new += [acc[m * 4 + t] + factor * lanes[t] for t in range(4)]
            return tuple(new)

        start = tuple(jnp.zeros((8, 128), F32) for _ in range(32))
        return jnp.concatenate(lax.fori_loop(0, 64, step, start, unroll=4), axis=0)

    def backward(rows, grad, source, to_lin, to_gate):
        both_d[:, :128] = (grad * to_lin[rows, :]).astype(BF16)
        both_d[:, 128:] = (grad * to_gate[rows, :]).astype(BF16)
        return lax.dot_general(
            source[rows, :], both_d[...], (((0,), (0,)), ((), ())), preferred_element_type=F32
        )

    weights[...] = jnp.zeros_like(weights)

    def add_weights(first, both):
        weights[first : first + 128, :] += both[:, :128]
        weights[first + 128 : first + 256, :] += both[:, 128:]

    @pl.loop(0, 8)
    def _(n):
        rows = pl.ds(pl.multiple_of(n * 256, 256), 256)
        grad = contract(lambda s, m: s * 64 + n * 8 + m, slab_value)
        add_weights(256, backward(rows, grad, pair_ref, pair_lin, pair_gate))
        grad_pair[rows, :] = lax.dot_general(
            both_d[...], both_b[...], (((1,), (1,)), ((), ())), preferred_element_type=F32
        ).astype(BF16)
        grad = contract(lambda s, m: (n * 8 + m) * 64 + s, pair_value)
        for m in range(2):
            owner = n * 2 + m
            partial[owner % 2, owner // 2] = grad[m * 128 : (m + 1) * 128, :].astype(BF16)
        add_weights(0, backward(rows, grad, slab_ref, slab_lin, slab_gate))


def local(grad_all, slab_all, pair_full, weights, mask_slab, mask_residue):
    wide = pltpu.VMEM((2048, 128), F32)
    return pl.pallas_call(
        local_kernel,
        out_shape=(
            jax.ShapeDtypeStruct((2048, 128), BF16),
            jax.ShapeDtypeStruct((2, 8, 128, 128), BF16),
            jax.ShapeDtypeStruct((512, 128), F32),
        ),
        in_specs=[VMEM] * 7 + [SMEM] * 2,
        out_specs=(VMEM,) * 3,
        scratch_shapes=[
            pltpu.VMEM((4096, 128), F32),
            pltpu.VMEM((128, 256), BF16),
            pltpu.VMEM((128, 256), BF16),
            wide, wide, wide, wide, wide, wide,
            pltpu.VMEM((256, 256), BF16),
        ],
        name="local",
    )(grad_all, slab_all, pair_full.reshape(2048, 128), *weights, mask_slab, mask_residue)


REDUCE_SENDS = 1 + 3 + 1 + 1 + 3 + 3 + 15 + 3 + 3 + 1


def reduce_kernel(
    partial, weights, slab_ref, wal, wag, mask_slab, mask_res,
    grad_slab, total,
    both, to_lin, to_gate, both_d,
    p_core, p_one, p_x, p_two, p_h,
    w_core, w_one, w_x, w_two, w_y, w_three, w_z,
    send_sems, p_sems, c_sem, x_sems, y_sems, z_sems, yg_sems, xg_sems, cg_sem,
):
    me = Here()
    depth = me.h * 8 + me.z

    def deep(d):
        place = (depth + d) % 16
        return me.at(z=place % 8, h=place // 8)

    twin = me.at(core=1 - me.core)
    far = me.at(h=1 - me.h)
    xs = [me.at(x=(me.x + d) % 4) for d in (1, 2, 3)]
    ys = [me.at(y=(me.y + d) % 4) for d in (1, 2, 3)]
    zs = [deep(d) for d in range(1, 16)]
    ready = greet([twin] + xs + ys + zs)

    both[:, :128], both[:, 128:] = wal[...], wag[...]
    keys = key_mask(mask_res, me.row * 32)
    flags = jnp.concatenate([keys * mask_slab[me.col * 4 + m].astype(F32) for m in range(4)], axis=0)
    _, lin, gate = gates(slab_ref[...], both[...], flags)
    to_lin[...] = lin
    to_gate[...] = gate

    ready()
    out = Sender(send_sems)
    out.send(weights.at[1 - me.core], w_core, c_sem.at[0], twin)
    out.send(partial.at[1 - me.core], p_core, p_sems.at[0], twin)

    out.recv(w_core, c_sem.at[0], twin)
    w_one[...] = weights[me.core] + w_core[...]
    for d in (1, 3, 2):
        out.send(w_one.at[(me.x + d) % 4], w_x.at[d - 1], x_sems.at[d - 1], xs[d - 1])
    out.recv(p_core, p_sems.at[0], twin)
    p_one[...] = (partial[me.core].astype(F32) + p_core[...].astype(F32)).astype(BF16)
    for d in (1, 3, 2):
        spot = pl.ds(((me.x + d) % 4) * 2, 2)
        out.send(p_one.at[spot], p_x.at[d - 1], p_sems.at[d], xs[d - 1])

    sums = w_one[me.x]
    for d in (1, 3, 2):
        out.recv(w_x.at[d - 1], x_sems.at[d - 1], twin)
        sums = sums + w_x[d - 1]
    w_two[...] = sums
    for d in (1, 3, 2):
        out.send(w_two.at[(me.y + d) % 4], w_y.at[d - 1], y_sems.at[d - 1], ys[d - 1])

    sums = p_one[pl.ds(me.x * 2, 2)].astype(F32)
    for d in (1, 3, 2):
        out.recv(p_x.at[d - 1], p_sems.at[d], twin)
        sums = sums + p_x[d - 1].astype(F32)
    p_two[...] = sums.astype(BF16)
    out.send(p_two.at[1 - me.h], p_h, p_sems.at[4], far)

    sums = w_two[me.y]
    for d in (1, 3, 2):
        out.recv(w_y.at[d - 1], y_sems.at[d - 1], twin)
        sums = sums + w_y[d - 1]
    w_three[...] = sums
    w_z[depth] = sums
    for d in (8, 7, 9, 6, 10, 5, 11, 4, 12, 3, 13, 2, 14, 1, 15):
        out.send(w_three, w_z.at[depth], z_sems.at[d - 1], zs[d - 1])

    for d in (1, 15, 2, 14, 3, 13, 4, 12, 5, 11, 6, 10, 7, 9, 8):
        out.recv(w_z.at[(depth + 16 - d) % 16], z_sems.at[d - 1], twin)
    sums = w_z[0]
    for n in range(1, 16):
        sums = sums + w_z[n]
    total[me.core, me.x, me.y] = sums * (1.0 / 1024.0)
    spot = total.at[me.core, me.x, me.y]
    for d in (1, 3, 2):
        out.send(spot, spot, yg_sems.at[d - 1], ys[d - 1])

    out.recv(p_h, p_sems.at[4], far)
    grad = (p_two[me.h].astype(F32) + p_h[...].astype(F32))
    both_d[:, :128] = (grad * to_lin[...]).astype(BF16)
    both_d[:, 128:] = (grad * to_gate[...]).astype(BF16)
    grad_slab[...] = lax.dot_general(
        both_d[...], both[...], (((1,), (1,)), ((), ())), preferred_element_type=F32
    ).astype(BF16)

    for d in (1, 3, 2):
        out.recv(total.at[me.core, me.x, (me.y + 4 - d) % 4], yg_sems.at[d - 1], twin)
    spot = total.at[me.core, me.x]
    for d in (1, 3, 2):
        out.send(spot, spot, xg_sems.at[d - 1], xs[d - 1])
    for d in (1, 3, 2):
        out.recv(total.at[me.core, (me.x + 4 - d) % 4], xg_sems.at[d - 1], twin)
    spot = total.at[me.core]
    out.send(spot, spot, cg_sem.at[0], twin)
    out.recv(total.at[1 - me.core], cg_sem.at[0], twin)
    out.finish()


def reduce(partial, weights, pair_slab, w_a_lin, w_a_gate, mask_slab, mask_residue):
    dma = pltpu.SemaphoreType.DMA
    grad_slab, total = pl.pallas_call(
        reduce_kernel,
        out_shape=(
            jax.ShapeDtypeStruct((128, 128), BF16),
            jax.ShapeDtypeStruct((2, 4, 4, 16, 128), F32),
        ),
        in_specs=[VMEM] * 5 + [SMEM] * 2,
        out_specs=(VMEM, VMEM),
        scratch_shapes=[
            pltpu.VMEM((128, 256), BF16),
            pltpu.VMEM((128, 128), F32),
            pltpu.VMEM((128, 128), F32),
            pltpu.VMEM((128, 256), BF16),
            pltpu.VMEM((8, 128, 128), BF16),
            pltpu.VMEM((8, 128, 128), BF16),
            pltpu.VMEM((3, 2, 128, 128), BF16),
            pltpu.VMEM((2, 128, 128), BF16),
            pltpu.VMEM((128, 128), BF16),
            pltpu.VMEM((4, 4, 16, 128), F32),
            pltpu.VMEM((4, 4, 16, 128), F32),
            pltpu.VMEM((3, 4, 16, 128), F32),
            pltpu.VMEM((4, 16, 128), F32),
            pltpu.VMEM((3, 16, 128), F32),
            pltpu.VMEM((16, 128), F32),
            pltpu.VMEM((16, 16, 128), F32),
            dma((REDUCE_SENDS,)), dma((5,)), dma((1,)), dma((3,)), dma((3,)), dma((15,)),
            dma((3,)), dma((3,)), dma((1,)),
        ],
        compiler_params=pltpu.CompilerParams(collective_id=1, has_side_effects=True),
        name="reduce",
    )(
        partial,
        weights.reshape(2, 4, 4, 16, 128),
        pair_slab.reshape(128, 128),
        w_a_lin,
        w_a_gate,
        mask_slab,
        mask_residue,
    )
    return grad_slab.reshape(4, 32, 128), total.reshape(4, 128, 128)


def on_device(
    pair_slab, pair_full, grad_out, w_a_lin, w_a_gate, w_b_lin, w_b_gate, mask_slab, mask_residue
):
    grad_all, slab_all = gather(grad_out, pair_slab)
    grad_pair, partial, weights = local(
        grad_all, slab_all, pair_full, (w_a_lin, w_a_gate, w_b_lin, w_b_gate), mask_slab, mask_residue
    )
    grad_slab, grad_weights = reduce(
        partial, weights, pair_slab, w_a_lin, w_a_gate, mask_slab, mask_residue
    )
    return (grad_slab, grad_pair.reshape(64, 32, 128), grad_weights)


def solution(mesh):
    return jax.shard_map(
        on_device,
        mesh=mesh,
        in_specs=(
            P("col", "row", None),
            P("col", "row", None),
            P("row", "col", None),
            P(),
            P(),
            P(),
            P(),
            P(),
            P(),
        ),
        out_specs=(P("col", "row", None), P("col", "row", None), P()),
        check_vma=False,
    )
```

```python
import jax
import jax.numpy as jnp
from jax import lax
from jax.experimental import pallas as pl
from jax.experimental.pallas import tpu as pltpu
from jax.sharding import PartitionSpec as P

MESH = pl.DeviceIdType.MESH
F32 = jnp.float32
BF16 = jnp.bfloat16
VMEM = pl.BlockSpec(memory_space=pltpu.VMEM)
SMEM = pl.BlockSpec(memory_space=pltpu.SMEM)


class Here:
    def __init__(self):
        row = lax.axis_index("row")
        col = lax.axis_index("col")
        self.row, self.col = row, col
        self.z, self.y = row // 4, row % 4
        self.x, self.h, self.core = col // 4, (col // 2) % 2, col % 2

    def at(self, z=None, y=None, x=None, h=None, core=None):
        z = self.z if z is None else z
        y = self.y if y is None else y
        x = self.x if x is None else x
        h = self.h if h is None else h
        core = self.core if core is None else core
        return (z * 4 + y, x * 4 + h * 2 + core)


class Sender:
    def __init__(self, send_sems, anyone):
        self.send_sems, self.anyone = send_sems, anyone
        self.started = []

    def send(self, src, dst, recv_sem, device):
        copy = pltpu.make_async_remote_copy(
            src_ref=src,
            dst_ref=dst,
            send_sem=self.send_sems.at[len(self.started)],
            recv_sem=recv_sem,
            device_id=device,
            device_id_type=MESH,
        )
        copy.start()
        self.started.append(copy)

    def recv(self, dst, recv_sem):
        pltpu.make_async_remote_copy(
            src_ref=dst,
            dst_ref=dst,
            send_sem=self.send_sems.at[0],
            recv_sem=recv_sem,
            device_id=self.anyone,
            device_id_type=MESH,
        ).wait_recv()

    def finish(self):
        for copy in self.started:
            copy.wait_send()


def key_mask(mask_ref, base):
    spots = lax.broadcasted_iota(jnp.int32, (32, 128), 0)
    flags = jnp.zeros((32, 128), F32)
    for k in range(32):
        flags = jnp.where(spots == k, mask_ref[base + k].astype(F32), flags)
    return flags


def gates(rows, both, flags):
    product = jnp.dot(rows, both, preferred_element_type=F32)
    linear, sigmoid = product[:, :128], jax.nn.sigmoid(product[:, 128:])
    to_linear = flags * sigmoid
    return to_linear * linear, to_linear, to_linear * linear * (1.0 - sigmoid)


SENDS = 7 + 24 + 15 + 5 + 32 + 15 + 1
NEAR = (1, 3, 2)
XY = tuple((dx, dy) for dx in range(4) for dy in range(4))[1:]


def whole_kernel(
    grad_ref, slab_own_ref, pair_ref, wal, wag, wbl, wbg, mask_slab, mask_res,
    grad_slab, grad_pair, total,
    grad_all, slab_all, wide,
    both_a, both_b, slab_value, slab_lin, slab_gate, pair_value, pair_lin, pair_gate,
    slab_grad, pair_grad, both_d, both_s, sum_a, sum_b, partial,
    p_core, p_one, p_x, p_two, p_h,
    weights, w_core, w_one, w_xy, w_two, w_z,
    send_sems, gz, gy, sh, sx, sc, p_sems, c_sem, xy_sems, z_sems, xyg_sems, cg_sem,
):
    me = Here()
    zg, zl = me.z // 4, me.z % 4
    depth = me.h * 8 + me.z

    def deep(d):
        place = (depth + d) % 16
        return me.at(z=place % 8, h=place // 8)

    group = [me.at(z=zg * 4 + (zl + d) % 4) for d in (1, 2, 3)]
    across = me.at(z=(1 - zg) * 4 + zl)
    ys = [me.at(y=(me.y + d) % 4) for d in (1, 2, 3)]
    xs = [me.at(x=(me.x + d) % 4) for d in (1, 2, 3)]
    xys = [me.at(x=(me.x + dx) % 4, y=(me.y + dy) % 4) for dx, dy in XY]
    zs = [deep(d) for d in range(1, 16)]
    far = me.at(h=1 - me.h)
    twin = me.at(core=1 - me.core)

    peers = [twin] + xys + zs
    barrier = pltpu.get_barrier_semaphore()
    for peer in peers:
        pl.semaphore_signal(barrier, inc=1, device_id=peer, device_id_type=MESH)

    both_a[:, :128], both_a[:, 128:] = wal[...], wag[...]
    both_b[:, :128], both_b[:, 128:] = wbl[...], wbg[...]
    keys = key_mask(mask_res, me.row * 32)

    def forward(n, first, mask, rows_ref, both, value, to_lin, to_gate):
        rows = pl.ds(pl.multiple_of(n * 256, 256), 256)
        flags = jnp.concatenate(
            [keys * mask[first + n * 8 + m].astype(F32) for m in range(8)], axis=0
        )
        val, lin, gate = gates(rows_ref(n), both[...], flags)
        value[rows, :] = val.astype(BF16).astype(F32)
        to_lin[rows, :] = lin
        to_gate[rows, :] = gate

    @pl.loop(0, 8)
    def _(n):
        rows = pl.ds(pl.multiple_of(n * 256, 256), 256)
        forward(n, me.col * 64, mask_res, lambda n: pair_ref[rows, :], both_b, pair_value, pair_lin, pair_gate)

    sum_a[...] = jnp.zeros_like(sum_a)
    sum_b[...] = jnp.zeros_like(sum_b)
    pl.semaphore_wait(barrier, len(peers))
    out = Sender(send_sems, twin)

    def z_of(t):
        side = zg if t < 4 else 1 - zg
        return side * 4 + (zl + 4 - t % 4) % 4

    def block(t, y=None):
        return grad_all.at[z_of(t) * 4 + (me.y if y is None else y)]

    def col_of(u, d, core=None):
        h = me.h if u == 0 else 1 - me.h
        return ((me.x + 4 - d) % 4) * 4 + h * 2 + (me.core if core is None else core)

    own = grad_all.at[me.row]
    slab_own = slab_all.at[me.col]
    out.send(slab_own_ref, slab_own, sh.at[0], far)
    out.send(grad_ref, own, gz.at[3], across)
    for d in NEAR:
        out.send(grad_ref, own, gz.at[d - 1], group[d - 1])
    for d in NEAR:
        out.send(grad_ref, own, gy.at[0, d - 1], ys[d - 1])
    for d in NEAR:
        out.send(slab_own_ref, slab_own, sx.at[0, d - 1], xs[d - 1])
    out.send(slab_own_ref, slab_own, sc.at[0, 0], twin)
    grad_all[me.row] = grad_ref[...]
    slab_all[me.col] = slab_own_ref[...]

    def spread(t):
        out.recv(block(t), gz.at[t - 1])
        if t == 4:
            for d in NEAR:
                out.send(block(t), block(t), gz.at[3 + d], group[d - 1])
        for d in NEAR:
            out.send(block(t), block(t), gy.at[t, d - 1], ys[d - 1])

    def slab_round(u):
        for d in NEAR:
            spot = slab_all.at[col_of(u, d)]
            out.recv(spot, sx.at[u, d - 1])
            out.send(spot, spot, sc.at[u, d], twin)

    def contract(scalar_rows, vectors, vector_row, steps, start, unroll):
        def step(s, acc):
            acc = list(acc)
            for scalar_row, base in zip(scalar_rows, vector_row):
                first = base(s)
                lanes = [vectors[pl.ds(pl.multiple_of(first + t * 8, 8), 8), :] for t in range(4)]
                for m in range(8):
                    factor = wide[pl.ds(scalar_row(s, m), 8, stride=0), :]
                    for t in range(4):
                        acc[m * 4 + t] = acc[m * 4 + t] + factor * lanes[t]
            return tuple(acc)

        return jnp.concatenate(lax.fori_loop(0, steps, step, start, unroll=unroll), axis=0)

    zeros = tuple(jnp.zeros((8, 128), F32) for _ in range(32))

    def slab_sum(t):
        for d in NEAR:
            out.recv(block(t, (me.y + 4 - d) % 4), gy.at[t, d - 1])
        z = z_of(t)
        wide[pl.ds(pl.multiple_of(z * 512, 512), 512), :] = (
            grad_all[pl.ds(z * 4, 4)].reshape(512, 128).astype(F32)
        )
        grad = contract(
            [lambda s, m: (z * 8 + m) * 64 + s], pair_value, [lambda s: s * 32], 64, zeros, 4
        )
        slab_grad[pl.ds(pl.multiple_of(z * 256, 256), 256), :] = grad
        rounded = grad.astype(BF16)
        partial[0, z] = rounded[:128, :]
        partial[1, z] = rounded[128:, :]

    def slab_back(t):
        z = z_of(t)
        rows = pl.ds(pl.multiple_of(z * 256, 256), 256)
        grad = slab_grad[rows, :]
        both_s[:, :128] = (grad * slab_lin[rows, :]).astype(BF16)
        both_s[:, 128:] = (grad * slab_gate[rows, :]).astype(BF16)
        source = slab_all[pl.ds(z * 2, 2)].reshape(256, 128)
        sum_a[...] += lax.dot_general(
            source, both_s[...], (((0,), (0,)), ((), ())), preferred_element_type=F32
        )

    def pair_pass(ts, first, last):
        zz = [z_of(t) for t in ts]

        @pl.loop(0, 8)
        def _(n):
            rows = pl.ds(pl.multiple_of(n * 256, 256), 256)
            start = zeros
            if not first:
                start = tuple(
                    pair_grad[pl.ds(pl.multiple_of(n * 256 + t * 8, 8), 8), :] for t in range(32)
                )
            grad = contract(
                [lambda s, m, z=z: (z * 8 + s) * 64 + n * 8 + m for z in zz],
                slab_value,
                [lambda s, z=z: (z * 8 + s) * 32 for z in zz],
                8,
                start,
                1 if len(ts) > 3 else (2 if len(ts) > 1 else 4),
            )
            if not last:
                pair_grad[rows, :] = grad
            else:
                both_d[rows, :128] = (grad * pair_lin[rows, :]).astype(BF16)
                both_d[rows, 128:] = (grad * pair_gate[rows, :]).astype(BF16)
                sum_b[...] += lax.dot_general(
                    pair_ref[rows, :], both_d[rows, :], (((0,), (0,)), ((), ())),
                    preferred_element_type=F32,
                )

    spread(1)
    spread(3)
    spread(2)
    slab_round(0)
    spread(4)
    slab_sum(0)
    slab_sum(1)
    slab_sum(3)
    spot = slab_all.at[col_of(1, 0)]
    out.recv(spot, sh.at[0])
    for d in NEAR:
        out.send(spot, spot, sx.at[1, d - 1], xs[d - 1])
    out.send(spot, spot, sc.at[1, 0], twin)
    spread(5)
    spread(7)
    slab_sum(2)
    spread(6)
    slab_round(1)
    slab_sum(4)
    for u in range(2):
        for d in range(4):
            out.recv(slab_all.at[col_of(u, d, 1 - me.core)], sc.at[u, d])

    @pl.loop(0, 8)
    def _(n):
        forward(
            n, 0, mask_slab, lambda n: slab_all[pl.ds(n * 2, 2)].reshape(256, 128), both_a,
            slab_value, slab_lin, slab_gate,
        )

    pair_pass((0, 1, 3, 2, 4), True, False)
    for t in (0, 1, 3, 2, 4):
        slab_back(t)
    slab_sum(5)
    slab_sum(7)
    slab_back(5)
    slab_back(7)
    pair_pass((5, 7), False, False)
    slab_sum(6)
    out.send(partial.at[1 - me.core], p_core, p_sems.at[0], twin)
    slab_back(6)
    pair_pass((6,), False, True)

    for n, acc in ((0, sum_a), (1, sum_b)):
        for side in range(2):
            half = acc[:, side * 128 : side * 128 + 128].reshape(8, 16, 128)
            weights[n, pl.ds(side * 8, 8)] = half
    out.send(weights.at[1 - me.core], w_core, c_sem.at[0], twin)

    out.recv(p_core, p_sems.at[0])
    p_one[...] = (partial[me.core].astype(F32) + p_core[...].astype(F32)).astype(BF16)
    for d in NEAR:
        spot = pl.ds(((me.x + d) % 4) * 2, 2)
        out.send(p_one.at[spot], p_x.at[d - 1], p_sems.at[d], xs[d - 1])

    out.recv(w_core, c_sem.at[0])
    w_one[...] = weights[me.core] + w_core[...]
    for n, (dx, dy) in enumerate(XY):
        part = ((me.x + dx) % 4) * 4 + (me.y + dy) % 4
        out.send(w_one.at[part], w_xy.at[n], xy_sems.at[n], xys[n])
    sums = w_one[me.x * 4 + me.y]
    for n in range(15):
        out.recv(w_xy.at[n], xy_sems.at[n])
        sums = sums + w_xy[n]
    w_two[...] = sums
    w_z[depth] = sums
    for d in (8, 7, 9, 6, 10, 5, 11, 4, 12, 3, 13, 2, 14, 1, 15):
        out.send(w_two, w_z.at[depth], z_sems.at[d - 1], zs[d - 1])

    sums = p_one[pl.ds(me.x * 2, 2)].astype(F32)
    for d in NEAR:
        out.recv(p_x.at[d - 1], p_sems.at[d])
        sums = sums + p_x[d - 1].astype(F32)
    p_two[...] = sums
    out.send(p_two.at[1 - me.h], p_h, p_sems.at[4], far)

    @pl.loop(0, 8)
    def _(n):
        rows = pl.ds(pl.multiple_of(n * 256, 256), 256)
        grad_pair[rows, :] = lax.dot_general(
            both_d[rows, :], both_b[...], (((1,), (1,)), ((), ())), preferred_element_type=F32
        ).astype(BF16)

    for d in (1, 15, 2, 14, 3, 13, 4, 12, 5, 11, 6, 10, 7, 9, 8):
        out.recv(w_z.at[(depth + 16 - d) % 16], z_sems.at[d - 1])
    sums = w_z[0]
    for n in range(1, 16):
        sums = sums + w_z[n]
    place = me.x * 4 + me.y
    total[me.core, place] = sums * (1.0 / 1024.0)
    spot = total.at[me.core, place]
    for n, (dx, dy) in enumerate(XY):
        out.send(spot, spot, xyg_sems.at[n], xys[n])

    out.recv(p_h, p_sems.at[4])
    grad = p_two[me.h] + p_h[...]
    rows = pl.ds(pl.multiple_of(me.col * 128, 128), 128)
    both_s[:128, :128] = (grad * slab_lin[rows, :]).astype(BF16)
    both_s[:128, 128:] = (grad * slab_gate[rows, :]).astype(BF16)
    grad_slab[...] = lax.dot_general(
        both_s[:128, :], both_a[...], (((1,), (1,)), ((), ())), preferred_element_type=F32
    ).astype(BF16)

    for n, (dx, dy) in enumerate(XY):
        part = ((me.x + 4 - dx) % 4) * 4 + (me.y + 4 - dy) % 4
        out.recv(total.at[me.core, part], xyg_sems.at[n])
    spot = total.at[me.core]
    out.send(spot, spot, cg_sem.at[0], twin)
    out.recv(total.at[1 - me.core], cg_sem.at[0])
    out.finish()


def on_device(
    pair_slab, pair_full, grad_out, w_a_lin, w_a_gate, w_b_lin, w_b_gate, mask_slab, mask_residue
):
    dma = pltpu.SemaphoreType.DMA
    rows_f32 = pltpu.VMEM((2048, 128), F32)
    grad_slab, grad_pair, total = pl.pallas_call(
        whole_kernel,
        out_shape=(
            jax.ShapeDtypeStruct((128, 128), BF16),
            jax.ShapeDtypeStruct((2048, 128), BF16),
            jax.ShapeDtypeStruct((2, 16, 16, 128), F32),
        ),
        in_specs=[VMEM] * 7 + [SMEM] * 2,
        out_specs=(VMEM,) * 3,
        scratch_shapes=[
            pltpu.VMEM((32, 2, 64, 128), BF16),
            pltpu.VMEM((16, 4, 32, 128), BF16),
            pltpu.VMEM((4096, 128), F32),
            pltpu.VMEM((128, 256), BF16),
            pltpu.VMEM((128, 256), BF16),
            rows_f32, rows_f32, rows_f32, rows_f32, rows_f32, rows_f32, rows_f32, rows_f32,
            pltpu.VMEM((2048, 256), BF16),
            pltpu.VMEM((256, 256), BF16),
            pltpu.VMEM((128, 256), F32),
            pltpu.VMEM((128, 256), F32),
            pltpu.VMEM((2, 8, 128, 128), BF16),
            pltpu.VMEM((8, 128, 128), BF16),
            pltpu.VMEM((8, 128, 128), BF16),
            pltpu.VMEM((3, 2, 128, 128), BF16),
            pltpu.VMEM((2, 128, 128), F32),
            pltpu.VMEM((128, 128), F32),
            pltpu.VMEM((2, 16, 16, 128), F32),
            pltpu.VMEM((16, 16, 128), F32),
            pltpu.VMEM((16, 16, 128), F32),
            pltpu.VMEM((15, 16, 128), F32),
            pltpu.VMEM((16, 128), F32),
            pltpu.VMEM((16, 16, 128), F32),
            dma((SENDS,)), dma((7,)), dma((8, 3)), dma((1,)), dma((2, 3)), dma((2, 4)),
            dma((5,)), dma((1,)), dma((15,)), dma((15,)), dma((15,)), dma((1,)),
        ],
        compiler_params=pltpu.CompilerParams(collective_id=0, has_side_effects=True),
        name="whole",
    )(
        grad_out, pair_slab, pair_full.reshape(2048, 128),
        w_a_lin, w_a_gate, w_b_lin, w_b_gate, mask_slab, mask_residue,
    )
    return (
        grad_slab.reshape(4, 32, 128),
        grad_pair.reshape(64, 32, 128),
        total.reshape(4, 128, 128),
    )


def solution(mesh):
    return jax.shard_map(
        on_device,
        mesh=mesh,
        in_specs=(
            P("col", "row", None),
            P("col", "row", None),
            P("row", "col", None),
            P(),
            P(),
            P(),
            P(),
            P(),
            P(),
        ),
        out_specs=(P("col", "row", None), P("col", "row", None), P()),
        check_vma=False,
    )
```

```python
import jax
import jax.numpy as jnp
from jax import lax
from jax.experimental import pallas as pl
from jax.experimental.pallas import tpu as pltpu
from jax.sharding import PartitionSpec as P

MESH = pl.DeviceIdType.MESH
F32 = jnp.float32
BF16 = jnp.bfloat16
VMEM = pl.BlockSpec(memory_space=pltpu.VMEM)
SMEM = pl.BlockSpec(memory_space=pltpu.SMEM)


class Here:
    def __init__(self):
        row = lax.axis_index("row")
        col = lax.axis_index("col")
        self.row, self.col = row, col
        self.z, self.y = row // 4, row % 4
        self.x, self.h, self.core = col // 4, (col // 2) % 2, col % 2

    def at(self, z=None, y=None, x=None, h=None, core=None):
        z = self.z if z is None else z
        y = self.y if y is None else y
        x = self.x if x is None else x
        h = self.h if h is None else h
        core = self.core if core is None else core
        return (z * 4 + y, x * 4 + h * 2 + core)


class Sender:
    def __init__(self, send_sems, anyone):
        self.send_sems, self.anyone = send_sems, anyone
        self.started = []

    def send(self, src, dst, recv_sem, device, only=None):
        copy = pltpu.make_async_remote_copy(
            src_ref=src,
            dst_ref=dst,
            send_sem=self.send_sems.at[len(self.started)],
            recv_sem=recv_sem,
            device_id=device,
            device_id_type=MESH,
        )
        if only is None:
            copy.start()
        else:
            pl.when(only)(copy.start)
        self.started.append((copy, only))

    def recv(self, dst, recv_sem):
        pltpu.make_async_remote_copy(
            src_ref=dst,
            dst_ref=dst,
            send_sem=self.send_sems.at[0],
            recv_sem=recv_sem,
            device_id=self.anyone,
            device_id_type=MESH,
        ).wait_recv()

    def finish(self):
        for copy, only in self.started:
            if only is None:
                copy.wait_send()
            else:
                pl.when(only)(copy.wait_send)


def key_mask(mask_ref, base):
    spots = lax.broadcasted_iota(jnp.int32, (32, 128), 0)
    flags = jnp.zeros((32, 128), F32)
    for k in range(32):
        flags = jnp.where(spots == k, mask_ref[base + k].astype(F32), flags)
    return flags


def gates(rows, both, flags):
    product = jnp.dot(rows, both, preferred_element_type=F32)
    linear, sigmoid = product[:, :128], jax.nn.sigmoid(product[:, 128:])
    to_linear = flags * sigmoid
    return to_linear * linear, to_linear, to_linear * linear * (1.0 - sigmoid)


SENDS = 7 + 24 + 15 + 8 + 8 + 1 + 1 + 15 + 15 + 15 + 16
NEAR = (1, 3, 2)
XY = tuple((dx, dy) for dx in range(4) for dy in range(4))[1:]


def whole_kernel(
    grad_ref, slab_own_ref, pair_ref, wal, wag, wbl, wbg, mask_slab, mask_res,
    grad_slab, grad_pair, total,
    grad_all, slab_all, wide,
    both_a, both_b, slab_value, slab_lin, slab_gate, pair_value, pair_lin, pair_gate,
    slab_grad, pair_grad, both_d, both_s, sum_a, sum_b, partial,
    p_core, p_wide, p_one, p_x, p_two, p_h,
    weights, w_core, w_one, w_xy, w_two, w_z,
    send_sems, gz, gy, sh, sx, sc, pc_sems, px_sems, ph_sem, c_sem, xy_sems, z_sems, xyg_sems, cg_sems,
):
    me = Here()
    zg, zl = me.z // 4, me.z % 4
    depth = me.h * 8 + me.z

    def deep(d):
        place = (depth + d) % 16
        return me.at(z=place % 8, h=place // 8)

    group = [me.at(z=zg * 4 + (zl + d) % 4) for d in (1, 2, 3)]
    across = me.at(z=(1 - zg) * 4 + zl)
    ys = [me.at(y=(me.y + d) % 4) for d in (1, 2, 3)]
    xs = [me.at(x=(me.x + d) % 4) for d in (1, 2, 3)]
    xys = [me.at(x=(me.x + dx) % 4, y=(me.y + dy) % 4) for dx, dy in XY]
    zs = [deep(d) for d in range(1, 16)]
    far = me.at(h=1 - me.h)
    twin = me.at(core=1 - me.core)

    peers = [twin] + xys + zs
    barrier = pltpu.get_barrier_semaphore()
    for peer in peers:
        pl.semaphore_signal(barrier, inc=1, device_id=peer, device_id_type=MESH)

    both_a[:, :128], both_a[:, 128:] = wal[...], wag[...]
    both_b[:, :128], both_b[:, 128:] = wbl[...], wbg[...]
    keys = key_mask(mask_res, me.row * 32)

    def forward(n, first, mask, rows_ref, both, value, to_lin, to_gate):
        rows = pl.ds(pl.multiple_of(n * 256, 256), 256)
        flags = jnp.concatenate(
            [keys * mask[first + n * 8 + m].astype(F32) for m in range(8)], axis=0
        )
        val, lin, gate = gates(rows_ref(n), both[...], flags)
        value[rows, :] = val.astype(BF16).astype(F32)
        to_lin[rows, :] = lin
        to_gate[rows, :] = gate

    @pl.loop(0, 8)
    def _(n):
        rows = pl.ds(pl.multiple_of(n * 256, 256), 256)
        forward(n, me.col * 64, mask_res, lambda n: pair_ref[rows, :], both_b, pair_value, pair_lin, pair_gate)

    sum_a[...] = jnp.zeros_like(sum_a)
    sum_b[...] = jnp.zeros_like(sum_b)
    pl.semaphore_wait(barrier, len(peers))
    out = Sender(send_sems, twin)

    def z_of(t):
        return (zg + t // 4) % 2 * 4 + (zl + 4 - t % 4) % 4

    def block(t, y=None):
        return grad_all.at[z_of(t) * 4 + (me.y if y is None else y)]

    def col_of(u, d, core=None):
        h = me.h if u == 0 else 1 - me.h
        return ((me.x + 4 - d) % 4) * 4 + h * 2 + (me.core if core is None else core)

    own = grad_all.at[me.row]
    slab_own = slab_all.at[me.col]
    out.send(slab_own_ref, slab_own, sh.at[0], far)
    out.send(grad_ref, own, gz.at[3], across)
    for d in NEAR:
        out.send(grad_ref, own, gz.at[d - 1], group[d - 1])
    for d in NEAR:
        out.send(grad_ref, own, gy.at[0, d - 1], ys[d - 1])
    for d in NEAR:
        out.send(slab_own_ref, slab_own, sx.at[0, d - 1], xs[d - 1])
    out.send(slab_own_ref, slab_own, sc.at[0, 0], twin)
    grad_all[me.row] = grad_ref[...]
    slab_all[me.col] = slab_own_ref[...]

    def spread(t):
        out.recv(block(t), gz.at[t - 1])
        if t == 4:
            for d in NEAR:
                out.send(block(t), block(t), gz.at[3 + d], group[d - 1])
        for d in NEAR:
            out.send(block(t), block(t), gy.at[t, d - 1], ys[d - 1])

    def slab_round(u):
        for d in NEAR:
            spot = slab_all.at[col_of(u, d)]
            out.recv(spot, sx.at[u, d - 1])
            out.send(spot, spot, sc.at[u, d], twin)

    def contract(scalar_rows, vectors, vector_row, steps, start, unroll):
        def step(s, acc):
            acc = list(acc)
            for scalar_row, base in zip(scalar_rows, vector_row):
                first = base(s)
                lanes = [vectors[pl.ds(pl.multiple_of(first + t * 8, 8), 8), :] for t in range(4)]
                for m in range(8):
                    factor = wide[pl.ds(scalar_row(s, m), 8, stride=0), :]
                    for t in range(4):
                        acc[m * 4 + t] = acc[m * 4 + t] + factor * lanes[t]
            return tuple(acc)

        return jnp.concatenate(lax.fori_loop(0, steps, step, start, unroll=unroll), axis=0)

    zeros = tuple(jnp.zeros((8, 128), F32) for _ in range(32))

    def slab_sum(t):
        for d in NEAR:
            out.recv(block(t, (me.y + 4 - d) % 4), gy.at[t, d - 1])
        z = z_of(t)
        wide[pl.ds(pl.multiple_of(z * 512, 512), 512), :] = (
            grad_all[pl.ds(z * 4, 4)].reshape(512, 128).astype(F32)
        )
        grad = contract(
            [lambda s, m: (z * 8 + m) * 64 + s], pair_value, [lambda s: s * 32], 64, zeros, 4
        )
        slab_grad[pl.ds(pl.multiple_of(z * 256, 256), 256), :] = grad
        rounded = grad.astype(BF16)
        partial[0, z] = rounded[:128, :]
        partial[1, z] = rounded[128:, :]
        out.send(partial.at[1 - me.core, z], p_core.at[z], pc_sems.at[t], twin)

    def slab_push(t):
        z = z_of(t)
        out.recv(p_core.at[z], pc_sems.at[t])
        mine = pl.ds(pl.multiple_of(z * 256 + me.core * 128, 128), 128)
        both = slab_grad[mine, :] + p_core[z].astype(F32)
        p_wide[z] = both
        p_one[z] = both.astype(BF16)
        d = (z // 2 + 4 - me.x) % 4
        slot = (d + 3) % 4 % 3
        out.send(
            p_one.at[z], p_x.at[slot, z % 2], px_sems.at[slot, z % 2], me.at(x=z // 2), d != 0
        )

    def slab_owner(h):
        sums = p_wide[me.x * 2 + h]
        for d in NEAR:
            out.recv(p_x.at[d - 1, h], px_sems.at[d - 1, h])
            sums = sums + p_x[d - 1, h].astype(F32)
        return sums

    def slab_back(t):
        z = z_of(t)
        rows = pl.ds(pl.multiple_of(z * 256, 256), 256)
        grad = slab_grad[rows, :]
        both_s[:, :128] = (grad * slab_lin[rows, :]).astype(BF16)
        both_s[:, 128:] = (grad * slab_gate[rows, :]).astype(BF16)
        source = slab_all[pl.ds(z * 2, 2)].reshape(256, 128)
        sum_a[...] += lax.dot_general(
            source, both_s[...], (((0,), (0,)), ((), ())), preferred_element_type=F32
        )

    def pair_pass(ts, first, last):
        zz = [z_of(t) for t in ts]

        @pl.loop(0, 8)
        def _(n):
            rows = pl.ds(pl.multiple_of(n * 256, 256), 256)
            start = zeros
            if not first:
                start = tuple(
                    pair_grad[pl.ds(pl.multiple_of(n * 256 + t * 8, 8), 8), :] for t in range(32)
                )
            grad = contract(
                [lambda s, m, z=z: (z * 8 + s) * 64 + n * 8 + m for z in zz],
                slab_value,
                [lambda s, z=z: (z * 8 + s) * 32 for z in zz],
                8,
                start,
                1 if len(ts) > 3 else (2 if len(ts) > 1 else 4),
            )
            if not last:
                pair_grad[rows, :] = grad
            else:
                both_d[rows, :128] = (grad * pair_lin[rows, :]).astype(BF16)
                both_d[rows, 128:] = (grad * pair_gate[rows, :]).astype(BF16)
                sum_b[...] += lax.dot_general(
                    pair_ref[rows, :], both_d[rows, :], (((0,), (0,)), ((), ())),
                    preferred_element_type=F32,
                )

    def slab_forward(h):
        for d in range(4):
            out.recv(slab_all.at[col_of(h, d, 1 - me.core)], sc.at[h, d])

        @pl.loop(0, 4)
        def _(n):
            forward(
                n * 2 + (me.h if h == 0 else 1 - me.h), 0, mask_slab,
                lambda n: slab_all[pl.ds(n * 2, 2)].reshape(256, 128), both_a,
                slab_value, slab_lin, slab_gate,
            )

    odd = (me.z + me.h) % 2
    spread(1)
    spread(3)
    spread(2)
    slab_round(0)
    slab_sum(0)
    spread(4)
    slab_forward(0)
    slab_sum(1)
    spot = slab_all.at[col_of(1, 0)]
    out.recv(spot, sh.at[0])
    for d in NEAR:
        out.send(spot, spot, sx.at[1, d - 1], xs[d - 1])
    out.send(spot, spot, sc.at[1, 0], twin)
    slab_push(0)
    slab_sum(3)
    spread(5)
    spread(7)
    spread(6)
    slab_push(1)
    slab_sum(2)
    slab_round(1)
    slab_push(3)
    pair_pass((odd, 2 + odd), True, False)
    slab_push(2)
    slab_sum(4)
    slab_forward(1)
    pair_pass((1 - odd, 3 - odd), False, False)
    for t in range(4):
        slab_back(t)
    slab_push(4)
    slab_sum(5)
    slab_back(4)
    slab_sum(7)
    slab_back(5)
    slab_push(5)
    pair_pass((4, 5, 7), False, False)
    slab_back(7)
    slab_push(7)
    slab_sum(6)
    slab_back(6)
    slab_push(6)
    pair_pass((6,), False, True)

    for n, acc in ((0, sum_a), (1, sum_b)):
        for side in range(2):
            half = acc[:, side * 128 : side * 128 + 128].reshape(8, 16, 128)
            weights[n, pl.ds(side * 8, 8)] = half
    out.send(weights.at[1 - me.core], w_core, c_sem.at[0], twin)

    out.recv(w_core, c_sem.at[0])
    w_one[...] = weights[me.core] + w_core[...]
    for n, (dx, dy) in enumerate(XY):
        part = ((me.x + dx) % 4) * 4 + (me.y + dy) % 4
        out.send(w_one.at[part], w_xy.at[n], xy_sems.at[n], xys[n])
    p_two[...] = slab_owner(1 - me.h)
    out.send(p_two, p_h, ph_sem.at[0], far)
    sums = w_one[me.x * 4 + me.y]
    for n in range(15):
        out.recv(w_xy.at[n], xy_sems.at[n])
        sums = sums + w_xy[n]
    w_two[...] = sums
    w_z[depth] = sums
    for d in (8, 7, 9, 6, 10, 5, 11, 4, 12, 3, 13, 2, 14, 1, 15):
        out.send(w_two, w_z.at[depth], z_sems.at[d - 1], zs[d - 1])


    @pl.loop(0, 8)
    def _(n):
        rows = pl.ds(pl.multiple_of(n * 256, 256), 256)
        grad_pair[rows, :] = lax.dot_general(
            both_d[rows, :], both_b[...], (((1,), (1,)), ((), ())), preferred_element_type=F32
        ).astype(BF16)

    for d in (1, 15, 2, 14, 3, 13, 4, 12, 5, 11, 6, 10, 7, 9, 8):
        out.recv(w_z.at[(depth + 16 - d) % 16], z_sems.at[d - 1])
    sums = w_z[0]
    for n in range(1, 16):
        sums = sums + w_z[n]
    place = me.x * 4 + me.y
    total[me.core, place] = sums * (1.0 / 1024.0)
    spot = total.at[me.core, place]
    for n, (dx, dy) in enumerate(XY):
        out.send(spot, spot, xyg_sems.at[n], xys[n])
    out.send(spot, spot, cg_sems.at[15], twin)

    grad = slab_owner(me.h)
    out.recv(p_h, ph_sem.at[0])
    grad = grad + p_h[...]
    rows = pl.ds(pl.multiple_of(me.col * 128, 128), 128)
    both_s[:128, :128] = (grad * slab_lin[rows, :]).astype(BF16)
    both_s[:128, 128:] = (grad * slab_gate[rows, :]).astype(BF16)
    grad_slab[...] = lax.dot_general(
        both_s[:128, :], both_a[...], (((1,), (1,)), ((), ())), preferred_element_type=F32
    ).astype(BF16)

    parts = [((me.x + 4 - dx) % 4) * 4 + (me.y + 4 - dy) % 4 for dx, dy in XY]
    for n in range(15):
        spot = total.at[me.core, parts[n]]
        out.recv(spot, xyg_sems.at[n])
        out.send(spot, spot, cg_sems.at[n], twin)
    for n in range(15):
        out.recv(total.at[1 - me.core, parts[n]], cg_sems.at[n])
    out.recv(total.at[1 - me.core, place], cg_sems.at[15])
    out.finish()


def on_device(
    pair_slab, pair_full, grad_out, w_a_lin, w_a_gate, w_b_lin, w_b_gate, mask_slab, mask_residue
):
    dma = pltpu.SemaphoreType.DMA
    rows_f32 = pltpu.VMEM((2048, 128), F32)
    grad_slab, grad_pair, total = pl.pallas_call(
        whole_kernel,
        out_shape=(
            jax.ShapeDtypeStruct((128, 128), BF16),
            jax.ShapeDtypeStruct((2048, 128), BF16),
            jax.ShapeDtypeStruct((2, 16, 16, 128), F32),
        ),
        in_specs=[VMEM] * 7 + [SMEM] * 2,
        out_specs=(VMEM,) * 3,
        scratch_shapes=[
            pltpu.VMEM((32, 2, 64, 128), BF16),
            pltpu.VMEM((16, 4, 32, 128), BF16),
            pltpu.VMEM((4096, 128), F32),
            pltpu.VMEM((128, 256), BF16),
            pltpu.VMEM((128, 256), BF16),
            rows_f32, rows_f32, rows_f32, rows_f32, rows_f32, rows_f32, rows_f32, rows_f32,
            pltpu.VMEM((2048, 256), BF16),
            pltpu.VMEM((256, 256), BF16),
            pltpu.VMEM((128, 256), F32),
            pltpu.VMEM((128, 256), F32),
            pltpu.VMEM((2, 8, 128, 128), BF16),
            pltpu.VMEM((8, 128, 128), BF16),
            pltpu.VMEM((8, 128, 128), F32),
            pltpu.VMEM((8, 128, 128), BF16),
            pltpu.VMEM((3, 2, 128, 128), BF16),
            pltpu.VMEM((128, 128), F32),
            pltpu.VMEM((128, 128), F32),
            pltpu.VMEM((2, 16, 16, 128), F32),
            pltpu.VMEM((16, 16, 128), F32),
            pltpu.VMEM((16, 16, 128), F32),
            pltpu.VMEM((15, 16, 128), F32),
            pltpu.VMEM((16, 128), F32),
            pltpu.VMEM((16, 16, 128), F32),
            dma((SENDS,)), dma((7,)), dma((8, 3)), dma((1,)), dma((2, 3)), dma((2, 4)),
            dma((8,)), dma((3, 2)), dma((1,)), dma((1,)), dma((15,)), dma((15,)), dma((15,)), dma((16,)),
        ],
        compiler_params=pltpu.CompilerParams(collective_id=0, has_side_effects=True),
        name="whole",
    )(
        grad_out, pair_slab, pair_full.reshape(2048, 128),
        w_a_lin, w_a_gate, w_b_lin, w_b_gate, mask_slab, mask_residue,
    )
    return (
        grad_slab.reshape(4, 32, 128),
        grad_pair.reshape(64, 32, 128),
        total.reshape(4, 128, 128),
    )


def solution(mesh):
    return jax.shard_map(
        on_device,
        mesh=mesh,
        in_specs=(
            P("col", "row", None),
            P("col", "row", None),
            P("row", "col", None),
            P(),
            P(),
            P(),
            P(),
            P(),
            P(),
        ),
        out_specs=(P("col", "row", None), P("col", "row", None), P()),
        check_vma=False,
    )
```

```python
import jax
import jax.numpy as jnp
from jax import lax
from jax.experimental import pallas as pl
from jax.experimental.pallas import tpu as pltpu
from jax.sharding import PartitionSpec as P

MESH = pl.DeviceIdType.MESH
F32 = jnp.float32
BF16 = jnp.bfloat16
ANY = pl.BlockSpec(memory_space=pl.ANY)


class Here:
    def __init__(self):
        row = lax.axis_index("row")
        col = lax.axis_index("col")
        self.row, self.col = row, col
        self.z, self.y = row // 4, row % 4
        self.x, self.h, self.core = col // 4, (col // 2) % 2, col % 2

    def at(self, z=None, y=None, x=None, h=None, core=None):
        z = self.z if z is None else z
        y = self.y if y is None else y
        x = self.x if x is None else x
        h = self.h if h is None else h
        core = self.core if core is None else core
        return (z * 4 + y, x * 4 + h * 2 + core)


class Sender:
    def __init__(self, send_sems, anyone):
        self.send_sems, self.anyone = send_sems, anyone
        self.started = []

    def send(self, src, dst, recv_sem, device, only=None):
        copy = pltpu.make_async_remote_copy(
            src_ref=src,
            dst_ref=dst,
            send_sem=self.send_sems.at[len(self.started)],
            recv_sem=recv_sem,
            device_id=device,
            device_id_type=MESH,
        )
        if only is None:
            copy.start()
        else:
            pl.when(only)(copy.start)
        self.started.append((copy, only))

    def recv(self, dst, recv_sem):
        pltpu.make_async_remote_copy(
            src_ref=dst,
            dst_ref=dst,
            send_sem=self.send_sems.at[0],
            recv_sem=recv_sem,
            device_id=self.anyone,
            device_id_type=MESH,
        ).wait_recv()

    def finish(self):
        for copy, only in self.started:
            if only is None:
                copy.wait_send()
            else:
                pl.when(only)(copy.wait_send)


def key_mask(mask_ref, base):
    spots = lax.broadcasted_iota(jnp.int32, (32, 128), 0)
    flags = jnp.zeros((32, 128), F32)
    for k in range(32):
        flags = jnp.where(spots == k, mask_ref[base + k].astype(F32), flags)
    return flags


def gates(rows, both, flags):
    product = jnp.dot(rows, both, preferred_element_type=F32)
    linear, sigmoid = product[:, :128], jax.nn.sigmoid(product[:, 128:])
    to_linear = flags * sigmoid
    return to_linear * linear, to_linear, to_linear * linear * (1.0 - sigmoid)


SENDS = 7 + 24 + 15 + 8 + 8 + 1 + 1 + 15 + 15 + 15 + 16
NEAR = (1, 3, 2)
XY = tuple((dx, dy) for dx in range(4) for dy in range(4))[1:]


def whole_kernel(
    grad_in, slab_in, pair_in, wal, wag, wbl, wbg, mask_slab_in, mask_res_in,
    grad_slab_out, grad_pair_out, total_out,
    pair_ref, mask_slab, mask_res, grad_slab, grad_pair, total, in_sems, out_sems,
    grad_all, slab_all, wide,
    both_a, both_b, slab_value, slab_lin, slab_gate, pair_value, pair_lin, pair_gate,
    slab_grad, pair_grad, both_d, both_s, sum_a, sum_b, partial,
    p_core, p_wide, p_one, p_x, p_two, p_h,
    weights, w_core, w_one, w_xy, w_two, w_z,
    send_sems, gz, gy, sh, sx, sc, pc_sems, px_sems, ph_sem, c_sem, xy_sems, z_sems, xyg_sems, cg_sems,
):
    me = Here()
    zg, zl = me.z // 4, me.z % 4
    depth = me.h * 8 + me.z

    def deep(d):
        place = (depth + d) % 16
        return me.at(z=place % 8, h=place // 8)

    group = [me.at(z=zg * 4 + (zl + d) % 4) for d in (1, 2, 3)]
    across = me.at(z=(1 - zg) * 4 + zl)
    ys = [me.at(y=(me.y + d) % 4) for d in (1, 2, 3)]
    xs = [me.at(x=(me.x + d) % 4) for d in (1, 2, 3)]
    xys = [me.at(x=(me.x + dx) % 4, y=(me.y + dy) % 4) for dx, dy in XY]
    zs = [deep(d) for d in range(1, 16)]
    far = me.at(h=1 - me.h)
    twin = me.at(core=1 - me.core)

    peers = [twin] + xys + [deep(d) for d in (1, 2, 3, 4, 12, 13, 14, 15)]
    barrier = pltpu.get_barrier_semaphore()
    for peer in peers:
        pl.semaphore_signal(barrier, inc=1, device_id=peer, device_id_type=MESH)

    own = grad_all.at[me.row]
    slab_own = slab_all.at[me.col]
    loads = [
        pltpu.make_async_copy(source, target, in_sems.at[n])
        for n, (source, target) in enumerate(
            (
                (mask_res_in, mask_res),
                (mask_slab_in, mask_slab),
                (wbl, both_b.at[:, pl.ds(0, 128)]),
                (wbg, both_b.at[:, pl.ds(128, 128)]),
                (pair_in, pair_ref),
                (grad_in, own),
                (slab_in, slab_own),
                (wal, both_a.at[:, pl.ds(0, 128)]),
                (wag, both_a.at[:, pl.ds(128, 128)]),
            )
        )
    ]
    for load in loads:
        load.start()
    for load in loads:
        load.wait()
    keys = key_mask(mask_res, me.row * 32)

    def forward(n, first, mask, rows_ref, both, value, to_lin, to_gate):
        rows = pl.ds(pl.multiple_of(n * 256, 256), 256)
        flags = jnp.concatenate(
            [keys * mask[first + n * 8 + m].astype(F32) for m in range(8)], axis=0
        )
        val, lin, gate = gates(rows_ref(n), both[...], flags)
        value[rows, :] = val.astype(BF16).astype(F32)
        to_lin[rows, :] = lin
        to_gate[rows, :] = gate

    @pl.loop(0, 8)
    def _(n):
        rows = pl.ds(pl.multiple_of(n * 256, 256), 256)
        forward(n, me.col * 64, mask_res, lambda n: pair_ref[rows, :], both_b, pair_value, pair_lin, pair_gate)

    sum_a[...] = jnp.zeros_like(sum_a)
    sum_b[...] = jnp.zeros_like(sum_b)
    pl.semaphore_wait(barrier, len(peers))
    out = Sender(send_sems, twin)

    def z_of(t):
        return (zg + t // 4) % 2 * 4 + (zl + 4 - t % 4) % 4

    def block(t, y=None):
        return grad_all.at[z_of(t) * 4 + (me.y if y is None else y)]

    def col_of(u, d, core=None):
        h = me.h if u == 0 else 1 - me.h
        return ((me.x + 4 - d) % 4) * 4 + h * 2 + (me.core if core is None else core)

    out.send(own, own, gz.at[3], across)
    for d in NEAR:
        out.send(own, own, gz.at[d - 1], group[d - 1])
    for d in NEAR:
        out.send(own, own, gy.at[0, d - 1], ys[d - 1])
    for d in NEAR:
        out.send(slab_own, slab_own, sx.at[0, d - 1], xs[d - 1])
    out.send(slab_own, slab_own, sc.at[0, 0], twin)

    def spread(t):
        out.recv(block(t), gz.at[t - 1])
        if t == 4:
            for d in NEAR:
                out.send(block(t), block(t), gz.at[3 + d], group[d - 1])
        for d in NEAR:
            out.send(block(t), block(t), gy.at[t, d - 1], ys[d - 1])

    def slab_round(u):
        for d in NEAR:
            spot = slab_all.at[col_of(u, d)]
            out.recv(spot, sx.at[u, d - 1])
            out.send(spot, spot, sc.at[u, d], twin)

    def contract(scalar_rows, vectors, vector_row, steps, start, unroll):
        def step(s, acc):
            acc = list(acc)
            for scalar_row, base in zip(scalar_rows, vector_row):
                first = base(s)
                lanes = [vectors[pl.ds(pl.multiple_of(first + t * 8, 8), 8), :] for t in range(4)]
                for m in range(8):
                    factor = wide[pl.ds(scalar_row(s, m), 8, stride=0), :]
                    for t in range(4):
                        acc[m * 4 + t] = acc[m * 4 + t] + factor * lanes[t]
            return tuple(acc)

        return jnp.concatenate(lax.fori_loop(0, steps, step, start, unroll=unroll), axis=0)

    zeros = tuple(jnp.zeros((8, 128), F32) for _ in range(32))

    def slab_sum(t):
        for d in NEAR:
            out.recv(block(t, (me.y + 4 - d) % 4), gy.at[t, d - 1])
        z = z_of(t)
        wide[pl.ds(pl.multiple_of(z * 512, 512), 512), :] = (
            grad_all[pl.ds(z * 4, 4)].reshape(512, 128).astype(F32)
        )
        grad = contract(
            [lambda s, m: (z * 8 + m) * 64 + s], pair_value, [lambda s: s * 32], 64, zeros, 4
        )
        slab_grad[pl.ds(pl.multiple_of(z * 256, 256), 256), :] = grad
        rounded = grad.astype(BF16)
        partial[0, z] = rounded[:128, :]
        partial[1, z] = rounded[128:, :]
        out.send(partial.at[1 - me.core, z], p_core.at[z], pc_sems.at[t], twin)

    def slab_push(t):
        z = z_of(t)
        out.recv(p_core.at[z], pc_sems.at[t])
        mine = pl.ds(pl.multiple_of(z * 256 + me.core * 128, 128), 128)
        both = slab_grad[mine, :] + p_core[z].astype(F32)
        p_wide[z] = both
        p_one[z] = both.astype(BF16)
        d = (z // 2 + 4 - me.x) % 4
        slot = (d + 3) % 4 % 3
        out.send(
            p_one.at[z], p_x.at[slot, z % 2], px_sems.at[slot, z % 2], me.at(x=z // 2), d != 0
        )

    def slab_owner(h):
        sums = p_wide[me.x * 2 + h]
        for d in NEAR:
            out.recv(p_x.at[d - 1, h], px_sems.at[d - 1, h])
            sums = sums + p_x[d - 1, h].astype(F32)
        return sums

    def slab_back(t):
        z = z_of(t)
        rows = pl.ds(pl.multiple_of(z * 256, 256), 256)
        grad = slab_grad[rows, :]
        both_s[:, :128] = (grad * slab_lin[rows, :]).astype(BF16)
        both_s[:, 128:] = (grad * slab_gate[rows, :]).astype(BF16)
        source = slab_all[pl.ds(z * 2, 2)].reshape(256, 128)
        sum_a[...] += lax.dot_general(
            source, both_s[...], (((0,), (0,)), ((), ())), preferred_element_type=F32
        )

    def pair_pass(ts, first, last):
        zz = [z_of(t) for t in ts]

        @pl.loop(0, 8)
        def _(n):
            rows = pl.ds(pl.multiple_of(n * 256, 256), 256)
            start = zeros
            if not first:
                start = tuple(
                    pair_grad[pl.ds(pl.multiple_of(n * 256 + t * 8, 8), 8), :] for t in range(32)
                )
            grad = contract(
                [lambda s, m, z=z: (z * 8 + s) * 64 + n * 8 + m for z in zz],
                slab_value,
                [lambda s, z=z: (z * 8 + s) * 32 for z in zz],
                8,
                start,
                1 if len(ts) > 3 else (2 if len(ts) > 1 else 4),
            )
            if not last:
                pair_grad[rows, :] = grad
            else:
                both_d[rows, :128] = (grad * pair_lin[rows, :]).astype(BF16)
                both_d[rows, 128:] = (grad * pair_gate[rows, :]).astype(BF16)
                sum_b[...] += lax.dot_general(
                    pair_ref[rows, :], both_d[rows, :], (((0,), (0,)), ((), ())),
                    preferred_element_type=F32,
                )

    def slab_forward(h):
        for d in range(4):
            out.recv(slab_all.at[col_of(h, d, 1 - me.core)], sc.at[h, d])

        @pl.loop(0, 4)
        def _(n):
            forward(
                n * 2 + (me.h if h == 0 else 1 - me.h), 0, mask_slab,
                lambda n: slab_all[pl.ds(n * 2, 2)].reshape(256, 128), both_a,
                slab_value, slab_lin, slab_gate,
            )

    odd = (me.z + me.h) % 2
    for t in (1, 3, 2):
        spread(t)
    slab_round(0)
    spread(4)
    out.send(slab_own, slab_own, sh.at[0], far)
    slab_sum(0)
    slab_forward(0)
    slab_sum(1)
    slab_sum(3)
    spread(5)
    spread(7)
    spread(6)
    slab_push(0)
    slab_push(1)
    slab_sum(2)
    pair_pass((odd, 2 + odd), True, False)
    slab_push(3)
    slab_push(2)
    slab_back(odd)
    slab_back(2 + odd)
    slab_sum(4)
    spot = slab_all.at[col_of(1, 0)]
    out.recv(spot, sh.at[0])
    for d in NEAR:
        out.send(spot, spot, sx.at[1, d - 1], xs[d - 1])
    out.send(spot, spot, sc.at[1, 0], twin)
    slab_sum(5)
    slab_sum(7)
    slab_push(4)
    slab_push(5)
    slab_sum(6)
    slab_push(7)
    pair_pass((4 + odd, 6 + odd), False, False)
    slab_push(6)
    slab_round(1)
    slab_back(4 + odd)
    slab_back(6 + odd)
    slab_forward(1)
    for t in (1, 3, 5, 7):
        slab_back(t - odd)
    pair_pass((1 - odd, 3 - odd, 5 - odd, 7 - odd), False, True)

    for n, acc in ((0, sum_a), (1, sum_b)):
        for side in range(2):
            half = acc[:, side * 128 : side * 128 + 128].reshape(8, 16, 128)
            weights[n, pl.ds(side * 8, 8)] = half
    out.send(weights.at[1 - me.core], w_core, c_sem.at[0], twin)

    out.recv(w_core, c_sem.at[0])
    w_one[...] = weights[me.core] + w_core[...]
    for n, (dx, dy) in enumerate(XY):
        part = ((me.x + dx) % 4) * 4 + (me.y + dy) % 4
        out.send(w_one.at[part], w_xy.at[n], xy_sems.at[n], xys[n])
    p_two[...] = slab_owner(1 - me.h)
    out.send(p_two, p_h, ph_sem.at[0], far)
    sums = w_one[me.x * 4 + me.y]
    for n in range(15):
        out.recv(w_xy.at[n], xy_sems.at[n])
        sums = sums + w_xy[n]
    w_two[...] = sums
    w_z[depth] = sums
    for d in (8, 7, 9, 6, 10, 5, 11, 4, 12, 3, 13, 2, 14, 1, 15):
        out.send(w_two, w_z.at[depth], z_sems.at[d - 1], zs[d - 1])


    @pl.loop(0, 8)
    def _(n):
        rows = pl.ds(pl.multiple_of(n * 256, 256), 256)
        grad_pair[rows, :] = lax.dot_general(
            both_d[rows, :], both_b[...], (((1,), (1,)), ((), ())), preferred_element_type=F32
        ).astype(BF16)

    stores = [pltpu.make_async_copy(grad_pair, grad_pair_out, out_sems.at[0])]
    stores[0].start()

    for d in (1, 15, 2, 14, 3, 13, 4, 12, 5, 11, 6, 10, 7, 9, 8):
        out.recv(w_z.at[(depth + 16 - d) % 16], z_sems.at[d - 1])
    sums = w_z[0]
    for n in range(1, 16):
        sums = sums + w_z[n]
    place = me.x * 4 + me.y
    total[me.core, place] = sums * (1.0 / 1024.0)
    spot = total.at[me.core, place]
    for n, (dx, dy) in enumerate(XY):
        out.send(spot, spot, xyg_sems.at[n], xys[n])
    out.send(spot, spot, cg_sems.at[15], twin)

    grad = slab_owner(me.h)
    out.recv(p_h, ph_sem.at[0])
    grad = grad + p_h[...]
    rows = pl.ds(pl.multiple_of(me.col * 128, 128), 128)
    both_s[:128, :128] = (grad * slab_lin[rows, :]).astype(BF16)
    both_s[:128, 128:] = (grad * slab_gate[rows, :]).astype(BF16)
    grad_slab[...] = lax.dot_general(
        both_s[:128, :], both_a[...], (((1,), (1,)), ((), ())), preferred_element_type=F32
    ).astype(BF16)
    stores.append(pltpu.make_async_copy(grad_slab, grad_slab_out, out_sems.at[1]))
    stores[1].start()

    parts = [((me.x + 4 - dx) % 4) * 4 + (me.y + 4 - dy) % 4 for dx, dy in XY]
    for n in range(15):
        spot = total.at[me.core, parts[n]]
        out.recv(spot, xyg_sems.at[n])
        out.send(spot, spot, cg_sems.at[n], twin)
    for n in range(15):
        out.recv(total.at[1 - me.core, parts[n]], cg_sems.at[n])
    out.recv(total.at[1 - me.core, place], cg_sems.at[15])
    stores.append(pltpu.make_async_copy(total, total_out, out_sems.at[2]))
    stores[2].start()
    out.finish()
    for store in stores:
        store.wait()


def settle_kernel(*refs):
    sources, targets, held, sems = refs[:3], refs[3:6], refs[6:9], refs[9]
    loads = [pltpu.make_async_copy(sources[n], held[n], sems.at[n]) for n in range(3)]
    for load in loads:
        load.start()
    stores = []
    for n in range(3):
        loads[n].wait()
        stores.append(pltpu.make_async_copy(held[n], targets[n], sems.at[3 + n]))
        stores[n].start()
    for store in stores:
        store.wait()


OUTS = (((128, 128), BF16), ((2048, 128), BF16), ((2, 16, 16, 128), F32))
SHAPES = tuple(jax.ShapeDtypeStruct(*out) for out in OUTS)
HELD = [pltpu.VMEM(*out) for out in OUTS]


def settle(*arrays):
    return pl.pallas_call(
        settle_kernel,
        out_shape=SHAPES,
        in_specs=[ANY] * 3,
        out_specs=(ANY,) * 3,
        scratch_shapes=HELD + [pltpu.SemaphoreType.DMA((6,))],
        name="settle",
    )(*arrays)


def on_device(
    pair_slab, pair_full, grad_out, w_a_lin, w_a_gate, w_b_lin, w_b_gate, mask_slab, mask_residue
):
    dma = pltpu.SemaphoreType.DMA
    rows_f32 = pltpu.VMEM((2048, 128), F32)
    grad_slab, grad_pair, total = pl.pallas_call(
        whole_kernel,
        out_shape=SHAPES,
        in_specs=[ANY] * 9,
        out_specs=(ANY,) * 3,
        scratch_shapes=[
            pltpu.VMEM((2048, 128), BF16),
            pltpu.SMEM((64,), jnp.int32),
            pltpu.SMEM((1024,), jnp.int32),
            *HELD,
            dma((9,)),
            dma((3,)),
            pltpu.VMEM((32, 2, 64, 128), BF16),
            pltpu.VMEM((16, 4, 32, 128), BF16),
            pltpu.VMEM((4096, 128), F32),
            pltpu.VMEM((128, 256), BF16),
            pltpu.VMEM((128, 256), BF16),
            rows_f32, rows_f32, rows_f32, rows_f32, rows_f32, rows_f32, rows_f32, rows_f32,
            pltpu.VMEM((2048, 256), BF16),
            pltpu.VMEM((256, 256), BF16),
            pltpu.VMEM((128, 256), F32),
            pltpu.VMEM((128, 256), F32),
            pltpu.VMEM((2, 8, 128, 128), BF16),
            pltpu.VMEM((8, 128, 128), BF16),
            pltpu.VMEM((8, 128, 128), F32),
            pltpu.VMEM((8, 128, 128), BF16),
            pltpu.VMEM((3, 2, 128, 128), BF16),
            pltpu.VMEM((128, 128), F32),
            pltpu.VMEM((128, 128), F32),
            pltpu.VMEM((2, 16, 16, 128), F32),
            pltpu.VMEM((16, 16, 128), F32),
            pltpu.VMEM((16, 16, 128), F32),
            pltpu.VMEM((15, 16, 128), F32),
            pltpu.VMEM((16, 128), F32),
            pltpu.VMEM((16, 16, 128), F32),
            dma((SENDS,)), dma((7,)), dma((8, 3)), dma((1,)), dma((2, 3)), dma((2, 4)),
            dma((8,)), dma((3, 2)), dma((1,)), dma((1,)), dma((15,)), dma((15,)), dma((15,)), dma((16,)),
        ],
        compiler_params=pltpu.CompilerParams(collective_id=0, has_side_effects=True),
        name="whole",
    )(
        grad_out, pair_slab, pair_full.reshape(2048, 128),
        w_a_lin, w_a_gate, w_b_lin, w_b_gate, mask_slab, mask_residue,
    )
    grad_slab, grad_pair, total = settle(grad_slab, grad_pair, total)
    return (
        grad_slab.reshape(4, 32, 128),
        grad_pair.reshape(64, 32, 128),
        total.reshape(4, 128, 128),
    )


def solution(mesh):
    return jax.shard_map(
        on_device,
        mesh=mesh,
        in_specs=(
            P("col", "row", None),
            P("col", "row", None),
            P("row", "col", None),
            P(),
            P(),
            P(),
            P(),
            P(),
            P(),
        ),
        out_specs=(P("col", "row", None), P("col", "row", None), P()),
        check_vma=False,
    )
```

```python
import jax
import jax.numpy as jnp
from jax import lax
from jax.experimental import pallas as pl
from jax.experimental.pallas import tpu as pltpu
from jax.sharding import PartitionSpec as P

MESH = pl.DeviceIdType.MESH
F32 = jnp.float32
BF16 = jnp.bfloat16
ANY = pl.BlockSpec(memory_space=pl.ANY)


class Here:
    def __init__(self):
        row = lax.axis_index("row")
        col = lax.axis_index("col")
        self.row, self.col = row, col
        self.z, self.y = row // 4, row % 4
        self.x, self.h, self.core = col // 4, (col // 2) % 2, col % 2

    def at(self, z=None, y=None, x=None, h=None, core=None):
        z = self.z if z is None else z
        y = self.y if y is None else y
        x = self.x if x is None else x
        h = self.h if h is None else h
        core = self.core if core is None else core
        return (z * 4 + y, x * 4 + h * 2 + core)


class Sender:
    def __init__(self, send_sems, anyone):
        self.send_sems, self.anyone = send_sems, anyone
        self.started = []

    def send(self, src, dst, recv_sem, device, only=None):
        copy = self.make(src, dst, recv_sem, device, only)
        if only is None:
            copy.start()
        else:
            pl.when(only)(copy.start)

    def make(self, src, dst, recv_sem, device, only=None):
        copy = pltpu.make_async_remote_copy(
            src_ref=src,
            dst_ref=dst,
            send_sem=self.send_sems.at[len(self.started)],
            recv_sem=recv_sem,
            device_id=device,
            device_id_type=MESH,
        )
        self.started.append((copy, only))
        return copy

    def recv(self, dst, recv_sem):
        pltpu.make_async_remote_copy(
            src_ref=dst,
            dst_ref=dst,
            send_sem=self.send_sems.at[0],
            recv_sem=recv_sem,
            device_id=self.anyone,
            device_id_type=MESH,
        ).wait_recv()

    def finish(self):
        for copy, only in self.started:
            if only is None:
                copy.wait_send()
            else:
                pl.when(only)(copy.wait_send)


def key_mask(mask_ref, base):
    spots = lax.broadcasted_iota(jnp.int32, (32, 128), 0)
    flags = jnp.zeros((32, 128), F32)
    for k in range(32):
        flags = jnp.where(spots == k, mask_ref[base + k].astype(F32), flags)
    return flags


def gates(rows, both, flags):
    product = jnp.dot(rows, both, preferred_element_type=F32)
    linear, sigmoid = product[:, :128], jax.nn.sigmoid(product[:, 128:])
    to_linear = flags * sigmoid
    return to_linear * linear, to_linear, to_linear * linear * (1.0 - sigmoid)


SENDS = 7 + 24 + 15 + 8 + 8 + 1 + 1 + 15 + 15 + 15 + 16
NEAR = (1, 3, 2)
XY = tuple((dx, dy) for dx in range(4) for dy in range(4))[1:]


def whole_kernel(
    grad_in, slab_in, pair_in, wal, wag, wbl, wbg, mask_slab_in, mask_res_in,
    grad_slab_out, grad_pair_out, total_out,
    pair_ref, mask_slab, mask_res, grad_slab, grad_pair, total, in_sems, out_sems,
    grad_all, slab_all, wide,
    both_a, both_b, slab_value, slab_lin, slab_gate, pair_value, pair_lin, pair_gate,
    slab_grad, pair_grad, both_d, both_s, sum_a, sum_b, partial,
    p_core, p_wide, p_one, p_x, p_two, p_h,
    weights, w_core, w_one, w_xy, w_two, w_z,
    send_sems, gz, gy, sh, sx, sc, pc_sems, px_sems, ph_sem, c_sem, xy_sems, z_sems, xyg_sems, cg_sems,
):
    me = Here()
    zg, zl = me.z // 4, me.z % 4
    depth = me.h * 8 + me.z

    def deep(d):
        place = (depth + d) % 16
        return me.at(z=place % 8, h=place // 8)

    group = [me.at(z=zg * 4 + (zl + d) % 4) for d in (1, 2, 3)]
    across = me.at(z=(1 - zg) * 4 + zl)
    ys = [me.at(y=(me.y + d) % 4) for d in (1, 2, 3)]
    xs = [me.at(x=(me.x + d) % 4) for d in (1, 2, 3)]
    xys = [me.at(x=(me.x + dx) % 4, y=(me.y + dy) % 4) for dx, dy in XY]
    zs = [deep(d) for d in range(1, 16)]
    far = me.at(h=1 - me.h)
    twin = me.at(core=1 - me.core)

    peers = [twin] + xys + [deep(d) for d in (1, 2, 3, 4, 12, 13, 14, 15)]
    barrier = pltpu.get_barrier_semaphore()
    for peer in peers:
        pl.semaphore_signal(barrier, inc=1, device_id=peer, device_id_type=MESH)

    own = grad_all.at[me.row]
    slab_own = slab_all.at[me.col]
    loads = [
        pltpu.make_async_copy(source, target, in_sems.at[n])
        for n, (source, target) in enumerate(
            (
                (mask_res_in, mask_res),
                (mask_slab_in, mask_slab),
                (wbl, both_b.at[:, pl.ds(0, 128)]),
                (wbg, both_b.at[:, pl.ds(128, 128)]),
                (pair_in, pair_ref),
                (grad_in, own),
                (slab_in, slab_own),
                (wal, both_a.at[:, pl.ds(0, 128)]),
                (wag, both_a.at[:, pl.ds(128, 128)]),
            )
        )
    ]
    for load in loads:
        load.start()
    for load in loads:
        load.wait()
    keys = key_mask(mask_res, me.row * 32)

    def forward(n, first, mask, rows_ref, both, value, to_lin, to_gate):
        rows = pl.ds(pl.multiple_of(n * 256, 256), 256)
        flags = jnp.concatenate(
            [keys * mask[first + n * 8 + m].astype(F32) for m in range(8)], axis=0
        )
        val, lin, gate = gates(rows_ref(n), both[...], flags)
        value[rows, :] = val.astype(BF16).astype(F32)
        to_lin[rows, :] = lin
        to_gate[rows, :] = gate

    @pl.loop(0, 8)
    def _(n):
        rows = pl.ds(pl.multiple_of(n * 256, 256), 256)
        forward(n, me.col * 64, mask_res, lambda n: pair_ref[rows, :], both_b, pair_value, pair_lin, pair_gate)

    sum_a[...] = jnp.zeros_like(sum_a)
    sum_b[...] = jnp.zeros_like(sum_b)
    pl.semaphore_wait(barrier, len(peers))
    out = Sender(send_sems, twin)

    def z_of(t):
        return (zg + t // 4) % 2 * 4 + (zl + 4 - t % 4) % 4

    def block(t, y=None):
        return grad_all.at[z_of(t) * 4 + (me.y if y is None else y)]

    def col_of(u, d, core=None):
        h = me.h if u == 0 else 1 - me.h
        return ((me.x + 4 - d) % 4) * 4 + h * 2 + (me.core if core is None else core)

    out.send(own, own, gz.at[3], across)
    for d in NEAR:
        out.send(own, own, gz.at[d - 1], group[d - 1])
    for d in NEAR:
        out.send(own, own, gy.at[0, d - 1], ys[d - 1])
    for d in NEAR:
        out.send(slab_own, slab_own, sx.at[0, d - 1], xs[d - 1])
    out.send(slab_own, slab_own, sc.at[0, 0], twin)

    def spread(t):
        out.recv(block(t), gz.at[t - 1])
        if t == 4:
            for d in NEAR:
                out.send(block(t), block(t), gz.at[3 + d], group[d - 1])
        for d in NEAR:
            out.send(block(t), block(t), gy.at[t, d - 1], ys[d - 1])

    def slab_round(u):
        for d in NEAR:
            spot = slab_all.at[col_of(u, d)]
            out.recv(spot, sx.at[u, d - 1])
            out.send(spot, spot, sc.at[u, d], twin)

    def contract(scalar_rows, vectors, vector_row, steps, start, unroll):
        def step(s, acc):
            acc = list(acc)
            for scalar_row, base in zip(scalar_rows, vector_row):
                first = base(s)
                lanes = [vectors[pl.ds(pl.multiple_of(first + t * 8, 8), 8), :] for t in range(4)]
                for m in range(8):
                    factor = wide[pl.ds(scalar_row(s, m), 8, stride=0), :]
                    for t in range(4):
                        acc[m * 4 + t] = acc[m * 4 + t] + factor * lanes[t]
            return tuple(acc)

        return jnp.concatenate(lax.fori_loop(0, steps, step, start, unroll=unroll), axis=0)

    zeros = tuple(jnp.zeros((8, 128), F32) for _ in range(32))

    def slab_sum(t):
        for d in NEAR:
            out.recv(block(t, (me.y + 4 - d) % 4), gy.at[t, d - 1])
        z = z_of(t)
        wide[pl.ds(pl.multiple_of(z * 512, 512), 512), :] = (
            grad_all[pl.ds(z * 4, 4)].reshape(512, 128).astype(F32)
        )
        grad = contract(
            [lambda s, m: (z * 8 + m) * 64 + s], pair_value, [lambda s: s * 32], 64, zeros, 4
        )
        slab_grad[pl.ds(pl.multiple_of(z * 256, 256), 256), :] = grad
        rounded = grad.astype(BF16)
        partial[0, z] = rounded[:128, :]
        partial[1, z] = rounded[128:, :]
        out.send(partial.at[1 - me.core, z], p_core.at[z], pc_sems.at[t], twin)

    def slab_push(t):
        z = z_of(t)
        out.recv(p_core.at[z], pc_sems.at[t])
        mine = pl.ds(pl.multiple_of(z * 256 + me.core * 128, 128), 128)
        both = slab_grad[mine, :] + p_core[z].astype(F32)
        p_wide[z] = both
        p_one[z] = both.astype(BF16)
        d = (z // 2 + 4 - me.x) % 4
        slot = (d + 3) % 4 % 3
        out.send(
            p_one.at[z], p_x.at[slot, z % 2], px_sems.at[slot, z % 2], me.at(x=z // 2), d != 0
        )

    def slab_owner(h):
        sums = p_wide[me.x * 2 + h]
        for d in NEAR:
            out.recv(p_x.at[d - 1, h], px_sems.at[d - 1, h])
            sums = sums + p_x[d - 1, h].astype(F32)
        return sums

    def slab_back(t):
        z = z_of(t)
        rows = pl.ds(pl.multiple_of(z * 256, 256), 256)
        grad = slab_grad[rows, :]
        both_s[:, :128] = (grad * slab_lin[rows, :]).astype(BF16)
        both_s[:, 128:] = (grad * slab_gate[rows, :]).astype(BF16)
        source = slab_all[pl.ds(z * 2, 2)].reshape(256, 128)
        sum_a[...] += lax.dot_general(
            source, both_s[...], (((0,), (0,)), ((), ())), preferred_element_type=F32
        )

    def pair_pass(ts, first, last, begin=0, end=8):
        zz = [z_of(t) for t in ts]

        @pl.loop(begin, end)
        def _(n):
            rows = pl.ds(pl.multiple_of(n * 256, 256), 256)
            start = zeros
            if not first:
                start = tuple(
                    pair_grad[pl.ds(pl.multiple_of(n * 256 + t * 8, 8), 8), :] for t in range(32)
                )
            grad = contract(
                [lambda s, m, z=z: (z * 8 + s) * 64 + n * 8 + m for z in zz],
                slab_value,
                [lambda s, z=z: (z * 8 + s) * 32 for z in zz],
                8,
                start,
                1 if len(ts) > 3 else (2 if len(ts) > 1 else 4),
            )
            if not last:
                pair_grad[rows, :] = grad
            else:
                both_d[rows, :128] = (grad * pair_lin[rows, :]).astype(BF16)
                both_d[rows, 128:] = (grad * pair_gate[rows, :]).astype(BF16)
                sum_b[...] += lax.dot_general(
                    pair_ref[rows, :], both_d[rows, :], (((0,), (0,)), ((), ())),
                    preferred_element_type=F32,
                )

    def slab_forward(h):
        for d in range(4):
            out.recv(slab_all.at[col_of(h, d, 1 - me.core)], sc.at[h, d])

        @pl.loop(0, 4)
        def _(n):
            forward(
                n * 2 + (me.h if h == 0 else 1 - me.h), 0, mask_slab,
                lambda n: slab_all[pl.ds(n * 2, 2)].reshape(256, 128), both_a,
                slab_value, slab_lin, slab_gate,
            )

    odd = (me.z + me.h) % 2
    for t in (1, 3, 2):
        spread(t)
    slab_round(0)
    spread(4)
    out.send(slab_own, slab_own, sh.at[0], far)
    slab_sum(0)
    slab_forward(0)
    slab_sum(1)
    slab_sum(3)
    spread(5)
    spread(7)
    spread(6)
    slab_push(0)
    slab_push(1)
    slab_sum(2)
    pair_pass((odd, 2 + odd), True, False)
    slab_push(3)
    slab_push(2)
    slab_back(odd)
    slab_back(2 + odd)
    slab_sum(4)
    spot = slab_all.at[col_of(1, 0)]
    out.recv(spot, sh.at[0])
    for d in NEAR:
        out.send(spot, spot, sx.at[1, d - 1], xs[d - 1])
    out.send(spot, spot, sc.at[1, 0], twin)
    slab_sum(5)
    slab_sum(7)
    slab_push(4)
    slab_push(5)
    slab_sum(6)
    slab_push(7)
    pair_pass((4 + odd, 6 + odd), False, False)
    slab_push(6)
    slab_round(1)
    slab_back(4 + odd)
    slab_back(6 + odd)
    slab_forward(1)
    for t in (1, 3, 5, 7):
        slab_back(t - odd)
    hand_over = out.make(weights.at[1 - me.core], w_core, c_sem.at[0], twin)
    scatter = [
        out.make(
            w_one.at[((me.x + dx) % 4) * 4 + (me.y + dy) % 4], w_xy.at[n], xy_sems.at[n], xys[n]
        )
        for n, (dx, dy) in enumerate(XY)
    ]

    def side_sums(n, acc):
        for part in range(2):
            half = acc[:, part * 128 : part * 128 + 128].reshape(8, 16, 128)
            weights[n, pl.ds(part * 8, 8)] = half
        pl.when(me.core != n)(hand_over.start)

    def side_scatter(n):
        @pl.when(me.core == n)
        def _():
            out.recv(w_core, c_sem.at[0])
            w_one[...] = weights[n] + w_core[...]
            for copy in scatter:
                copy.start()

    last = (1 - odd, 3 - odd, 5 - odd, 7 - odd)
    side_sums(0, sum_a)
    pair_pass(last, False, True, 0, 4)
    side_scatter(0)
    p_two[...] = slab_owner(1 - me.h)
    out.send(p_two, p_h, ph_sem.at[0], far)
    pair_pass(last, False, True, 4, 8)
    side_sums(1, sum_b)
    side_scatter(1)
    sums = w_one[me.x * 4 + me.y]
    for n in range(15):
        out.recv(w_xy.at[n], xy_sems.at[n])
        sums = sums + w_xy[n]
    w_two[...] = sums
    w_z[depth] = sums
    for d in (8, 7, 9, 6, 10, 5, 11, 4, 12, 3, 13, 2, 14, 1, 15):
        out.send(w_two, w_z.at[depth], z_sems.at[d - 1], zs[d - 1])


    @pl.loop(0, 8)
    def _(n):
        rows = pl.ds(pl.multiple_of(n * 256, 256), 256)
        grad_pair[rows, :] = lax.dot_general(
            both_d[rows, :], both_b[...], (((1,), (1,)), ((), ())), preferred_element_type=F32
        ).astype(BF16)

    stores = [pltpu.make_async_copy(grad_pair, grad_pair_out, out_sems.at[0])]
    stores[0].start()

    for d in (1, 15, 2, 14, 3, 13, 4, 12, 5, 11, 6, 10, 7, 9, 8):
        out.recv(w_z.at[(depth + 16 - d) % 16], z_sems.at[d - 1])
    sums = w_z[0]
    for n in range(1, 16):
        sums = sums + w_z[n]
    place = me.x * 4 + me.y
    total[me.core, place] = sums * (1.0 / 1024.0)
    spot = total.at[me.core, place]
    for n, (dx, dy) in enumerate(XY):
        out.send(spot, spot, xyg_sems.at[n], xys[n])
    out.send(spot, spot, cg_sems.at[15], twin)

    grad = slab_owner(me.h)
    out.recv(p_h, ph_sem.at[0])
    grad = grad + p_h[...]
    rows = pl.ds(pl.multiple_of(me.col * 128, 128), 128)
    both_s[:128, :128] = (grad * slab_lin[rows, :]).astype(BF16)
    both_s[:128, 128:] = (grad * slab_gate[rows, :]).astype(BF16)
    grad_slab[...] = lax.dot_general(
        both_s[:128, :], both_a[...], (((1,), (1,)), ((), ())), preferred_element_type=F32
    ).astype(BF16)
    stores.append(pltpu.make_async_copy(grad_slab, grad_slab_out, out_sems.at[1]))
    stores[1].start()

    parts = [((me.x + 4 - dx) % 4) * 4 + (me.y + 4 - dy) % 4 for dx, dy in XY]
    for n in range(15):
        spot = total.at[me.core, parts[n]]
        out.recv(spot, xyg_sems.at[n])
        out.send(spot, spot, cg_sems.at[n], twin)
    for n in range(15):
        out.recv(total.at[1 - me.core, parts[n]], cg_sems.at[n])
    out.recv(total.at[1 - me.core, place], cg_sems.at[15])
    stores.append(pltpu.make_async_copy(total, total_out, out_sems.at[2]))
    stores[2].start()
    out.finish()
    for store in stores:
        store.wait()


def settle_kernel(*refs):
    sources, targets, held, sems = refs[:3], refs[3:6], refs[6:9], refs[9]
    loads = [pltpu.make_async_copy(sources[n], held[n], sems.at[n]) for n in range(3)]
    for load in loads:
        load.start()
    stores = []
    for n in range(3):
        loads[n].wait()
        stores.append(pltpu.make_async_copy(held[n], targets[n], sems.at[3 + n]))
        stores[n].start()
    for store in stores:
        store.wait()


OUTS = (((128, 128), BF16), ((2048, 128), BF16), ((2, 16, 16, 128), F32))
SHAPES = tuple(jax.ShapeDtypeStruct(*out) for out in OUTS)
HELD = [pltpu.VMEM(*out) for out in OUTS]


def settle(*arrays):
    return pl.pallas_call(
        settle_kernel,
        out_shape=SHAPES,
        in_specs=[ANY] * 3,
        out_specs=(ANY,) * 3,
        scratch_shapes=HELD + [pltpu.SemaphoreType.DMA((6,))],
        name="settle",
    )(*arrays)


def on_device(
    pair_slab, pair_full, grad_out, w_a_lin, w_a_gate, w_b_lin, w_b_gate, mask_slab, mask_residue
):
    dma = pltpu.SemaphoreType.DMA
    rows_f32 = pltpu.VMEM((2048, 128), F32)
    grad_slab, grad_pair, total = pl.pallas_call(
        whole_kernel,
        out_shape=SHAPES,
        in_specs=[ANY] * 9,
        out_specs=(ANY,) * 3,
        scratch_shapes=[
            pltpu.VMEM((2048, 128), BF16),
            pltpu.SMEM((64,), jnp.int32),
            pltpu.SMEM((1024,), jnp.int32),
            *HELD,
            dma((9,)),
            dma((3,)),
            pltpu.VMEM((32, 2, 64, 128), BF16),
            pltpu.VMEM((16, 4, 32, 128), BF16),
            pltpu.VMEM((4096, 128), F32),
            pltpu.VMEM((128, 256), BF16),
            pltpu.VMEM((128, 256), BF16),
            rows_f32, rows_f32, rows_f32, rows_f32, rows_f32, rows_f32, rows_f32, rows_f32,
            pltpu.VMEM((2048, 256), BF16),
            pltpu.VMEM((256, 256), BF16),
            pltpu.VMEM((128, 256), F32),
            pltpu.VMEM((128, 256), F32),
            pltpu.VMEM((2, 8, 128, 128), BF16),
            pltpu.VMEM((8, 128, 128), BF16),
            pltpu.VMEM((8, 128, 128), F32),
            pltpu.VMEM((8, 128, 128), BF16),
            pltpu.VMEM((3, 2, 128, 128), BF16),
            pltpu.VMEM((128, 128), F32),
            pltpu.VMEM((128, 128), F32),
            pltpu.VMEM((2, 16, 16, 128), F32),
            pltpu.VMEM((16, 16, 128), F32),
            pltpu.VMEM((16, 16, 128), F32),
            pltpu.VMEM((15, 16, 128), F32),
            pltpu.VMEM((16, 128), F32),
            pltpu.VMEM((16, 16, 128), F32),
            dma((SENDS,)), dma((7,)), dma((8, 3)), dma((1,)), dma((2, 3)), dma((2, 4)),
            dma((8,)), dma((3, 2)), dma((1,)), dma((1,)), dma((15,)), dma((15,)), dma((15,)), dma((16,)),
        ],
        compiler_params=pltpu.CompilerParams(collective_id=0, has_side_effects=True),
        name="whole",
    )(
        grad_out, pair_slab, pair_full.reshape(2048, 128),
        w_a_lin, w_a_gate, w_b_lin, w_b_gate, mask_slab, mask_residue,
    )
    grad_slab, grad_pair, total = settle(grad_slab, grad_pair, total)
    return (
        grad_slab.reshape(4, 32, 128),
        grad_pair.reshape(64, 32, 128),
        total.reshape(4, 128, 128),
    )


def solution(mesh):
    return jax.shard_map(
        on_device,
        mesh=mesh,
        in_specs=(
            P("col", "row", None),
            P("col", "row", None),
            P("row", "col", None),
            P(),
            P(),
            P(),
            P(),
            P(),
            P(),
        ),
        out_specs=(P("col", "row", None), P("col", "row", None), P()),
        check_vma=False,
    )
```

```python
import jax
import jax.numpy as jnp
from jax import lax
from jax.experimental import pallas as pl
from jax.experimental.pallas import tpu as pltpu
from jax.sharding import PartitionSpec as P

MESH = pl.DeviceIdType.MESH
F32 = jnp.float32
BF16 = jnp.bfloat16
ANY = pl.BlockSpec(memory_space=pl.ANY)


class Here:
    def __init__(self):
        row = lax.axis_index("row")
        col = lax.axis_index("col")
        self.row, self.col = row, col
        self.z, self.y = row // 4, row % 4
        self.x, self.h, self.core = col // 4, (col // 2) % 2, col % 2

    def at(self, z=None, y=None, x=None, h=None, core=None):
        z = self.z if z is None else z
        y = self.y if y is None else y
        x = self.x if x is None else x
        h = self.h if h is None else h
        core = self.core if core is None else core
        return (z * 4 + y, x * 4 + h * 2 + core)


class Sender:
    def __init__(self, send_sems, anyone):
        self.send_sems, self.anyone = send_sems, anyone
        self.started = []

    def send(self, src, dst, recv_sem, device, only=None):
        copy = self.make(src, dst, recv_sem, device, only)
        if only is None:
            copy.start()
        else:
            pl.when(only)(copy.start)

    def make(self, src, dst, recv_sem, device, only=None):
        copy = pltpu.make_async_remote_copy(
            src_ref=src,
            dst_ref=dst,
            send_sem=self.send_sems.at[len(self.started)],
            recv_sem=recv_sem,
            device_id=device,
            device_id_type=MESH,
        )
        self.started.append((copy, only))
        return copy

    def recv(self, dst, recv_sem):
        pltpu.make_async_remote_copy(
            src_ref=dst,
            dst_ref=dst,
            send_sem=self.send_sems.at[0],
            recv_sem=recv_sem,
            device_id=self.anyone,
            device_id_type=MESH,
        ).wait_recv()

    def finish(self):
        for copy, only in self.started:
            if only is None:
                copy.wait_send()
            else:
                pl.when(only)(copy.wait_send)


def key_mask(mask_ref, base):
    spots = lax.broadcasted_iota(jnp.int32, (32, 128), 0)
    flags = jnp.zeros((32, 128), F32)
    for k in range(32):
        flags = jnp.where(spots == k, mask_ref[base + k].astype(F32), flags)
    return flags


def gates(rows, both, flags):
    product = jnp.dot(rows, both, preferred_element_type=F32)
    linear, sigmoid = product[:, :128], jax.nn.sigmoid(product[:, 128:])
    to_linear = flags * sigmoid
    return to_linear * linear, to_linear, to_linear * linear * (1.0 - sigmoid)


SENDS = 7 + 24 + 15 + 8 + 8 + 1 + 1 + 15 + 15 + 15 + 16
NEAR = (1, 3, 2)
XY = tuple((dx, dy) for dx in range(4) for dy in range(4))[1:]


def whole_kernel(
    grad_in, slab_in, pair_in, wal, wag, wbl, wbg, mask_slab_in, mask_res_in,
    grad_slab, grad_pair, total,
    pair_ref, mask_slab, mask_res, in_sems,
    grad_all, slab_all, wide,
    both_a, both_b, slab_value, slab_lin, slab_gate, pair_value, pair_lin, pair_gate,
    slab_grad, pair_grad, both_d, both_s, sum_a, sum_b, partial,
    p_core, p_wide, p_one, p_x, p_two, p_h,
    weights, w_core, w_one, w_xy, w_two, w_z,
    send_sems, gz, gy, sh, sx, sc, pc_sems, px_sems, ph_sem, c_sem, xy_sems, z_sems, xyg_sems, cg_sems,
):
    me = Here()
    zg, zl = me.z // 4, me.z % 4
    depth = me.h * 8 + me.z

    def deep(d):
        place = (depth + d) % 16
        return me.at(z=place % 8, h=place // 8)

    group = [me.at(z=zg * 4 + (zl + d) % 4) for d in (1, 2, 3)]
    across = me.at(z=(1 - zg) * 4 + zl)
    ys = [me.at(y=(me.y + d) % 4) for d in (1, 2, 3)]
    xs = [me.at(x=(me.x + d) % 4) for d in (1, 2, 3)]
    xys = [me.at(x=(me.x + dx) % 4, y=(me.y + dy) % 4) for dx, dy in XY]
    zs = [deep(d) for d in range(1, 16)]
    far = me.at(h=1 - me.h)
    twin = me.at(core=1 - me.core)

    peers = [twin] + xys + [deep(d) for d in (1, 2, 3, 4, 12, 13, 14, 15)]
    barrier = pltpu.get_barrier_semaphore()
    for peer in peers:
        pl.semaphore_signal(barrier, inc=1, device_id=peer, device_id_type=MESH)

    own = grad_all.at[me.row]
    slab_own = slab_all.at[me.col]
    loads = [
        pltpu.make_async_copy(source, target, in_sems.at[n])
        for n, (source, target) in enumerate(
            (
                (mask_res_in, mask_res),
                (mask_slab_in, mask_slab),
                (wbl, both_b.at[:, pl.ds(0, 128)]),
                (wbg, both_b.at[:, pl.ds(128, 128)]),
                (pair_in, pair_ref),
                (grad_in, own),
                (slab_in, slab_own),
                (wal, both_a.at[:, pl.ds(0, 128)]),
                (wag, both_a.at[:, pl.ds(128, 128)]),
            )
        )
    ]
    for load in loads:
        load.start()
    for load in loads:
        load.wait()
    keys = key_mask(mask_res, me.row * 32)

    def forward(n, first, mask, rows_ref, both, value, to_lin, to_gate):
        rows = pl.ds(pl.multiple_of(n * 256, 256), 256)
        flags = jnp.concatenate(
            [keys * mask[first + n * 8 + m].astype(F32) for m in range(8)], axis=0
        )
        val, lin, gate = gates(rows_ref(n), both[...], flags)
        value[rows, :] = val.astype(BF16).astype(F32)
        to_lin[rows, :] = lin
        to_gate[rows, :] = gate

    @pl.loop(0, 8)
    def _(n):
        rows = pl.ds(pl.multiple_of(n * 256, 256), 256)
        forward(n, me.col * 64, mask_res, lambda n: pair_ref[rows, :], both_b, pair_value, pair_lin, pair_gate)

    sum_a[...] = jnp.zeros_like(sum_a)
    sum_b[...] = jnp.zeros_like(sum_b)
    pl.semaphore_wait(barrier, len(peers))
    out = Sender(send_sems, twin)

    def z_of(t):
        return (zg + t // 4) % 2 * 4 + (zl + 4 - t % 4) % 4

    def block(t, y=None):
        return grad_all.at[z_of(t) * 4 + (me.y if y is None else y)]

    def col_of(u, d, core=None):
        h = me.h if u == 0 else 1 - me.h
        return ((me.x + 4 - d) % 4) * 4 + h * 2 + (me.core if core is None else core)

    out.send(own, own, gz.at[3], across)
    for d in NEAR:
        out.send(own, own, gz.at[d - 1], group[d - 1])
    for d in NEAR:
        out.send(own, own, gy.at[0, d - 1], ys[d - 1])
    for d in NEAR:
        out.send(slab_own, slab_own, sx.at[0, d - 1], xs[d - 1])
    out.send(slab_own, slab_own, sc.at[0, 0], twin)

    def spread(t):
        out.recv(block(t), gz.at[t - 1])
        if t == 4:
            for d in (2, 1, 3):
                out.send(block(t), block(t), gz.at[3 + d], group[d - 1])
        for d in (2, 1, 3):
            out.send(block(t), block(t), gy.at[t, d - 1], ys[d - 1])

    def slab_round(u):
        for d in NEAR:
            spot = slab_all.at[col_of(u, d)]
            out.recv(spot, sx.at[u, d - 1])
            out.send(spot, spot, sc.at[u, d], twin)

    def contract(scalar_rows, vectors, vector_row, steps, start, unroll):
        def step(s, acc):
            acc = list(acc)
            for scalar_row, base in zip(scalar_rows, vector_row):
                first = base(s)
                lanes = [vectors[pl.ds(pl.multiple_of(first + t * 8, 8), 8), :] for t in range(4)]
                for m in range(8):
                    factor = wide[pl.ds(scalar_row(s, m), 8, stride=0), :]
                    for t in range(4):
                        acc[m * 4 + t] = acc[m * 4 + t] + factor * lanes[t]
            return tuple(acc)

        return jnp.concatenate(lax.fori_loop(0, steps, step, start, unroll=unroll), axis=0)

    zeros = tuple(jnp.zeros((8, 128), F32) for _ in range(32))

    def slab_sum(t):
        for d in NEAR:
            out.recv(block(t, (me.y + 4 - d) % 4), gy.at[t, d - 1])
        z = z_of(t)
        wide[pl.ds(pl.multiple_of(z * 512, 512), 512), :] = (
            grad_all[pl.ds(z * 4, 4)].reshape(512, 128).astype(F32)
        )
        grad = contract(
            [lambda s, m: (z * 8 + m) * 64 + s], pair_value, [lambda s: s * 32], 64, zeros, 4
        )
        slab_grad[pl.ds(pl.multiple_of(z * 256, 256), 256), :] = grad
        rounded = grad.astype(BF16)
        partial[0, z] = rounded[:128, :]
        partial[1, z] = rounded[128:, :]
        out.send(partial.at[1 - me.core, z], p_core.at[z], pc_sems.at[t], twin)

    def slab_push(t):
        z = z_of(t)
        out.recv(p_core.at[z], pc_sems.at[t])
        mine = pl.ds(pl.multiple_of(z * 256 + me.core * 128, 128), 128)
        both = slab_grad[mine, :] + p_core[z].astype(F32)
        p_wide[z] = both
        p_one[z] = both.astype(BF16)
        d = (z // 2 + 4 - me.x) % 4
        slot = (d + 3) % 4 % 3
        out.send(
            p_one.at[z], p_x.at[slot, z % 2], px_sems.at[slot, z % 2], me.at(x=z // 2), d != 0
        )

    def slab_owner(h):
        sums = p_wide[me.x * 2 + h]
        for d in NEAR:
            out.recv(p_x.at[d - 1, h], px_sems.at[d - 1, h])
            sums = sums + p_x[d - 1, h].astype(F32)
        return sums

    def slab_back(t):
        z = z_of(t)
        rows = pl.ds(pl.multiple_of(z * 256, 256), 256)
        grad = slab_grad[rows, :]
        both_s[:, :128] = (grad * slab_lin[rows, :]).astype(BF16)
        both_s[:, 128:] = (grad * slab_gate[rows, :]).astype(BF16)
        source = slab_all[pl.ds(z * 2, 2)].reshape(256, 128)
        sum_a[...] += lax.dot_general(
            source, both_s[...], (((0,), (0,)), ((), ())), preferred_element_type=F32
        )

    def pair_pass(ts, first, last, begin=0, end=8):
        zz = [z_of(t) for t in ts]

        @pl.loop(begin, end)
        def _(n):
            rows = pl.ds(pl.multiple_of(n * 256, 256), 256)
            start = zeros
            if not first:
                start = tuple(
                    pair_grad[pl.ds(pl.multiple_of(n * 256 + t * 8, 8), 8), :] for t in range(32)
                )
            grad = contract(
                [lambda s, m, z=z: (z * 8 + s) * 64 + n * 8 + m for z in zz],
                slab_value,
                [lambda s, z=z: (z * 8 + s) * 32 for z in zz],
                8,
                start,
                1 if len(ts) > 3 else (2 if len(ts) > 1 else 4),
            )
            if not last:
                pair_grad[rows, :] = grad
            else:
                both_d[rows, :128] = (grad * pair_lin[rows, :]).astype(BF16)
                both_d[rows, 128:] = (grad * pair_gate[rows, :]).astype(BF16)
                sum_b[...] += lax.dot_general(
                    pair_ref[rows, :], both_d[rows, :], (((0,), (0,)), ((), ())),
                    preferred_element_type=F32,
                )

    def slab_forward(h):
        for d in range(4):
            out.recv(slab_all.at[col_of(h, d, 1 - me.core)], sc.at[h, d])

        @pl.loop(0, 4)
        def _(n):
            forward(
                n * 2 + (me.h if h == 0 else 1 - me.h), 0, mask_slab,
                lambda n: slab_all[pl.ds(n * 2, 2)].reshape(256, 128), both_a,
                slab_value, slab_lin, slab_gate,
            )

    odd = (me.z + me.h) % 2
    for t in (1, 3, 2):
        spread(t)
    slab_round(0)
    spread(4)
    out.send(slab_own, slab_own, sh.at[0], far)
    slab_sum(0)
    slab_forward(0)
    slab_sum(1)
    slab_sum(3)
    spread(5)
    spread(7)
    spread(6)
    slab_push(0)
    slab_push(1)
    slab_sum(2)
    pair_pass((odd, 2 + odd), True, False)
    slab_push(3)
    slab_push(2)
    slab_back(odd)
    slab_back(2 + odd)
    slab_sum(4)
    spot = slab_all.at[col_of(1, 0)]
    out.recv(spot, sh.at[0])
    for d in NEAR:
        out.send(spot, spot, sx.at[1, d - 1], xs[d - 1])
    out.send(spot, spot, sc.at[1, 0], twin)
    slab_sum(5)
    slab_sum(7)
    slab_push(4)
    slab_push(5)
    slab_sum(6)
    slab_push(7)
    pair_pass((4 + odd, 6 + odd), False, False)
    slab_push(6)
    slab_round(1)
    slab_back(4 + odd)
    slab_back(6 + odd)
    slab_forward(1)
    for t in (1, 3, 5, 7):
        slab_back(t - odd)
    hand_over = out.make(weights.at[1 - me.core], w_core, c_sem.at[0], twin)
    scatter = [
        out.make(
            w_one.at[((me.x + dx) % 4) * 4 + (me.y + dy) % 4], w_xy.at[n], xy_sems.at[n], xys[n]
        )
        for n, (dx, dy) in enumerate(XY)
    ]

    def side_sums(n, acc):
        for part in range(2):
            half = acc[:, part * 128 : part * 128 + 128].reshape(8, 16, 128)
            weights[n, pl.ds(part * 8, 8)] = half
        pl.when(me.core != n)(hand_over.start)

    def side_scatter(n):
        @pl.when(me.core == n)
        def _():
            out.recv(w_core, c_sem.at[0])
            w_one[...] = weights[n] + w_core[...]
            for copy in scatter:
                copy.start()

    last = (1 - odd, 3 - odd, 5 - odd, 7 - odd)
    side_sums(0, sum_a)
    pair_pass(last, False, True, 0, 4)
    side_scatter(0)
    p_two[...] = slab_owner(1 - me.h)
    out.send(p_two, p_h, ph_sem.at[0], far)
    pair_pass(last, False, True, 4, 8)
    side_sums(1, sum_b)
    side_scatter(1)
    sums = w_one[me.x * 4 + me.y]
    for n in range(15):
        out.recv(w_xy.at[n], xy_sems.at[n])
        sums = sums + w_xy[n]
    w_two[...] = sums
    w_z[depth] = sums
    for d in (8, 7, 9, 6, 10, 5, 11, 4, 12, 3, 13, 2, 14, 1, 15):
        out.send(w_two, w_z.at[depth], z_sems.at[d - 1], zs[d - 1])


    @pl.loop(0, 8)
    def _(n):
        rows = pl.ds(pl.multiple_of(n * 256, 256), 256)
        grad_pair[rows, :] = lax.dot_general(
            both_d[rows, :], both_b[...], (((1,), (1,)), ((), ())), preferred_element_type=F32
        ).astype(BF16)

    for d in (1, 15, 2, 14, 3, 13, 4, 12, 5, 11, 6, 10, 7, 9, 8):
        out.recv(w_z.at[(depth + 16 - d) % 16], z_sems.at[d - 1])
    sums = w_z[0]
    for n in range(1, 16):
        sums = sums + w_z[n]
    place = me.x * 4 + me.y
    total[me.core, place] = sums * (1.0 / 1024.0)
    spot = total.at[me.core, place]
    for n, (dx, dy) in enumerate(XY):
        out.send(spot, spot, xyg_sems.at[n], xys[n])
    out.send(spot, spot, cg_sems.at[15], twin)

    grad = slab_owner(me.h)
    out.recv(p_h, ph_sem.at[0])
    grad = grad + p_h[...]
    rows = pl.ds(pl.multiple_of(me.col * 128, 128), 128)
    both_s[:128, :128] = (grad * slab_lin[rows, :]).astype(BF16)
    both_s[:128, 128:] = (grad * slab_gate[rows, :]).astype(BF16)
    grad_slab[...] = lax.dot_general(
        both_s[:128, :], both_a[...], (((1,), (1,)), ((), ())), preferred_element_type=F32
    ).astype(BF16)

    parts = [((me.x + 4 - dx) % 4) * 4 + (me.y + 4 - dy) % 4 for dx, dy in XY]
    for n in range(15):
        spot = total.at[me.core, parts[n]]
        out.recv(spot, xyg_sems.at[n])
        out.send(spot, spot, cg_sems.at[n], twin)
    for n in range(15):
        out.recv(total.at[1 - me.core, parts[n]], cg_sems.at[n])
    out.recv(total.at[1 - me.core, place], cg_sems.at[15])
    out.finish()


def settle_kernel(*refs):
    sources, targets, sems = refs[:3], refs[3:6], refs[6]
    stores = [pltpu.make_async_copy(sources[n], targets[n], sems.at[n]) for n in range(3)]
    for store in stores:
        store.start()
    for store in stores:
        store.wait()


OUTS = (((128, 128), BF16), ((2048, 128), BF16), ((2, 16, 16, 128), F32))
SHAPES = tuple(jax.ShapeDtypeStruct(*out) for out in OUTS)
HELD = tuple(pltpu.VMEM(*out) for out in OUTS)
VMEM = pl.BlockSpec(memory_space=pltpu.VMEM)


def settle(*arrays):
    return pl.pallas_call(
        settle_kernel,
        out_shape=SHAPES,
        in_specs=[ANY] * 3,
        out_specs=(ANY,) * 3,
        scratch_shapes=[pltpu.SemaphoreType.DMA((3,))],
        name="settle",
    )(*(pltpu.with_memory_space_constraint(a, pltpu.VMEM) for a in arrays))


def on_device(
    pair_slab, pair_full, grad_out, w_a_lin, w_a_gate, w_b_lin, w_b_gate, mask_slab, mask_residue
):
    dma = pltpu.SemaphoreType.DMA
    rows_f32 = pltpu.VMEM((2048, 128), F32)
    grad_slab, grad_pair, total = pl.pallas_call(
        whole_kernel,
        out_shape=HELD,
        in_specs=[ANY] * 9,
        out_specs=(VMEM,) * 3,
        scratch_shapes=[
            pltpu.VMEM((2048, 128), BF16),
            pltpu.SMEM((64,), jnp.int32),
            pltpu.SMEM((1024,), jnp.int32),
            dma((9,)),
            pltpu.VMEM((32, 2, 64, 128), BF16),
            pltpu.VMEM((16, 4, 32, 128), BF16),
            pltpu.VMEM((4096, 128), F32),
            pltpu.VMEM((128, 256), BF16),
            pltpu.VMEM((128, 256), BF16),
            rows_f32, rows_f32, rows_f32, rows_f32, rows_f32, rows_f32, rows_f32, rows_f32,
            pltpu.VMEM((2048, 256), BF16),
            pltpu.VMEM((256, 256), BF16),
            pltpu.VMEM((128, 256), F32),
            pltpu.VMEM((128, 256), F32),
            pltpu.VMEM((2, 8, 128, 128), BF16),
            pltpu.VMEM((8, 128, 128), BF16),
            pltpu.VMEM((8, 128, 128), F32),
            pltpu.VMEM((8, 128, 128), BF16),
            pltpu.VMEM((3, 2, 128, 128), BF16),
            pltpu.VMEM((128, 128), F32),
            pltpu.VMEM((128, 128), F32),
            pltpu.VMEM((2, 16, 16, 128), F32),
            pltpu.VMEM((16, 16, 128), F32),
            pltpu.VMEM((16, 16, 128), F32),
            pltpu.VMEM((15, 16, 128), F32),
            pltpu.VMEM((16, 128), F32),
            pltpu.VMEM((16, 16, 128), F32),
            dma((SENDS,)), dma((7,)), dma((8, 3)), dma((1,)), dma((2, 3)), dma((2, 4)),
            dma((8,)), dma((3, 2)), dma((1,)), dma((1,)), dma((15,)), dma((15,)), dma((15,)), dma((16,)),
        ],
        compiler_params=pltpu.CompilerParams(collective_id=0, has_side_effects=True),
        name="whole",
    )(
        grad_out, pair_slab, pair_full.reshape(2048, 128),
        w_a_lin, w_a_gate, w_b_lin, w_b_gate, mask_slab, mask_residue,
    )
    grad_slab, grad_pair, total = settle(grad_slab, grad_pair, total)
    return (
        grad_slab.reshape(4, 32, 128),
        grad_pair.reshape(64, 32, 128),
        total.reshape(4, 128, 128),
    )


def solution(mesh):
    return jax.shard_map(
        on_device,
        mesh=mesh,
        in_specs=(
            P("col", "row", None),
            P("col", "row", None),
            P("row", "col", None),
            P(),
            P(),
            P(),
            P(),
            P(),
            P(),
        ),
        out_specs=(P("col", "row", None), P("col", "row", None), P()),
        check_vma=False,
    )
```

```python
import jax
import jax.numpy as jnp
from jax import lax
from jax.experimental import pallas as pl
from jax.experimental.pallas import tpu as pltpu
from jax.sharding import PartitionSpec as P

MESH = pl.DeviceIdType.MESH
F32 = jnp.float32
BF16 = jnp.bfloat16
ANY = pl.BlockSpec(memory_space=pl.ANY)


class Here:
    def __init__(self):
        row = lax.axis_index("row")
        col = lax.axis_index("col")
        self.row, self.col = row, col
        self.z, self.y = row // 4, row % 4
        self.x, self.h, self.core = col // 4, (col // 2) % 2, col % 2

    def at(self, z=None, y=None, x=None, h=None, core=None):
        z = self.z if z is None else z
        y = self.y if y is None else y
        x = self.x if x is None else x
        h = self.h if h is None else h
        core = self.core if core is None else core
        return (z * 4 + y, x * 4 + h * 2 + core)


class Sender:
    def __init__(self, send_sems, anyone):
        self.send_sems, self.anyone = send_sems, anyone
        self.started = []

    def send(self, src, dst, recv_sem, device, only=None):
        copy = self.make(src, dst, recv_sem, device, only)
        if only is None:
            copy.start()
        else:
            pl.when(only)(copy.start)

    def make(self, src, dst, recv_sem, device, only=None):
        copy = pltpu.make_async_remote_copy(
            src_ref=src,
            dst_ref=dst,
            send_sem=self.send_sems.at[len(self.started)],
            recv_sem=recv_sem,
            device_id=device,
            device_id_type=MESH,
        )
        self.started.append((copy, only))
        return copy

    def recv(self, dst, recv_sem):
        pltpu.make_async_remote_copy(
            src_ref=dst,
            dst_ref=dst,
            send_sem=self.send_sems.at[0],
            recv_sem=recv_sem,
            device_id=self.anyone,
            device_id_type=MESH,
        ).wait_recv()

    def finish(self):
        for copy, only in self.started:
            if only is None:
                copy.wait_send()
            else:
                pl.when(only)(copy.wait_send)


def key_mask(mask_ref, base):
    spots = lax.broadcasted_iota(jnp.int32, (32, 128), 0)
    flags = jnp.zeros((32, 128), F32)
    for k in range(32):
        flags = jnp.where(spots == k, mask_ref[base + k].astype(F32), flags)
    return flags


def gates(rows, both, flags):
    product = jnp.dot(rows, both, preferred_element_type=F32)
    linear, sigmoid = product[:, :128], jax.nn.sigmoid(product[:, 128:])
    to_linear = flags * sigmoid
    return to_linear * linear, to_linear, to_linear * linear * (1.0 - sigmoid)


SENDS = 7 + 24 + 15 + 8 + 8 + 1 + 1 + 15 + 15 + 15 + 16
NEAR = (1, 3, 2)
XY = tuple((dx, dy) for dx in range(4) for dy in range(4))[1:]


def whole_kernel(
    grad_in, slab_in, pair_in, wal, wag, wbl, wbg, mask_slab_in, mask_res_in,
    grad_slab, grad_pair, total,
    pair_ref, mask_slab, mask_res, in_sems,
    grad_all, slab_all, wide,
    both_a, both_b, slab_value, slab_lin, slab_gate, pair_value, pair_lin, pair_gate,
    slab_grad, pair_grad, both_d, both_s, sum_a, sum_b, partial,
    p_core, p_wide, p_one, p_x, p_two, p_h,
    weights, w_core, w_one, w_xy, w_two, w_z,
    send_sems, gz, gy, sh, sx, sc, pc_sems, px_sems, ph_sem, c_sem, xy_sems, z_sems, xyg_sems, cg_sems,
):
    me = Here()
    zg, zl = me.z // 4, me.z % 4
    depth = me.h * 8 + me.z

    def deep(d):
        place = (depth + d) % 16
        return me.at(z=place % 8, h=place // 8)

    group = [me.at(z=zg * 4 + (zl + d) % 4) for d in (1, 2, 3)]
    across = me.at(z=(1 - zg) * 4 + zl)
    ys = [me.at(y=(me.y + d) % 4) for d in (1, 2, 3)]
    xs = [me.at(x=(me.x + d) % 4) for d in (1, 2, 3)]
    xys = [me.at(x=(me.x + dx) % 4, y=(me.y + dy) % 4) for dx, dy in XY]
    zs = [deep(d) for d in range(1, 16)]
    far = me.at(h=1 - me.h)
    twin = me.at(core=1 - me.core)

    peers = [twin] + xys + [deep(d) for d in (1, 2, 3, 4, 12, 13, 14, 15)]
    barrier = pltpu.get_barrier_semaphore()
    for peer in peers:
        pl.semaphore_signal(barrier, inc=1, device_id=peer, device_id_type=MESH)

    own = grad_all.at[me.row]
    slab_own = slab_all.at[me.col]
    loads = [
        pltpu.make_async_copy(source, target, in_sems.at[n])
        for n, (source, target) in enumerate(
            (
                (slab_in, slab_own),
                (grad_in, own),
                (mask_res_in, mask_res),
                (mask_slab_in, mask_slab),
                (wbl, both_b.at[:, pl.ds(0, 128)]),
                (wbg, both_b.at[:, pl.ds(128, 128)]),
                (pair_in, pair_ref),
                (wal, both_a.at[:, pl.ds(0, 128)]),
                (wag, both_a.at[:, pl.ds(128, 128)]),
            )
        )
    ]
    for load in loads:
        load.start()
    pl.semaphore_wait(barrier, len(peers))
    for load in loads[:2]:
        load.wait()
    out = Sender(send_sems, twin)

    def z_of(t):
        return (zg + t // 4) % 2 * 4 + (zl + 4 - t % 4) % 4

    def block(t, y=None):
        return grad_all.at[z_of(t) * 4 + (me.y if y is None else y)]

    def col_of(u, d, core=None):
        h = me.h if u == 0 else 1 - me.h
        return ((me.x + 4 - d) % 4) * 4 + h * 2 + (me.core if core is None else core)

    out.send(own, own, gz.at[3], across)
    for d in NEAR:
        out.send(own, own, gz.at[d - 1], group[d - 1])
    for d in NEAR:
        out.send(own, own, gy.at[0, d - 1], ys[d - 1])
    for d in NEAR:
        out.send(slab_own, slab_own, sx.at[0, d - 1], xs[d - 1])
    out.send(slab_own, slab_own, sc.at[0, 0], twin)

    for load in loads[2:]:
        load.wait()
    keys = key_mask(mask_res, me.row * 32)

    def forward(n, first, mask, rows_ref, both, value, to_lin, to_gate):
        rows = pl.ds(pl.multiple_of(n * 256, 256), 256)
        flags = jnp.concatenate(
            [keys * mask[first + n * 8 + m].astype(F32) for m in range(8)], axis=0
        )
        val, lin, gate = gates(rows_ref(n), both[...], flags)
        value[rows, :] = val.astype(BF16).astype(F32)
        to_lin[rows, :] = lin
        to_gate[rows, :] = gate

    @pl.loop(0, 8)
    def _(n):
        rows = pl.ds(pl.multiple_of(n * 256, 256), 256)
        forward(n, me.col * 64, mask_res, lambda n: pair_ref[rows, :], both_b, pair_value, pair_lin, pair_gate)

    sum_a[...] = jnp.zeros_like(sum_a)
    sum_b[...] = jnp.zeros_like(sum_b)
    def spread(t):
        out.recv(block(t), gz.at[t - 1])
        if t == 4:
            for d in (2, 1, 3):
                out.send(block(t), block(t), gz.at[3 + d], group[d - 1])
        for d in (2, 1, 3):
            out.send(block(t), block(t), gy.at[t, d - 1], ys[d - 1])

    def slab_round(u):
        for d in NEAR:
            spot = slab_all.at[col_of(u, d)]
            out.recv(spot, sx.at[u, d - 1])
            out.send(spot, spot, sc.at[u, d], twin)

    def contract(scalar_rows, vectors, vector_row, steps, start, unroll):
        def step(s, acc):
            acc = list(acc)
            for scalar_row, base in zip(scalar_rows, vector_row):
                first = base(s)
                lanes = [vectors[pl.ds(pl.multiple_of(first + t * 8, 8), 8), :] for t in range(4)]
                for m in range(8):
                    factor = wide[pl.ds(scalar_row(s, m), 8, stride=0), :]
                    for t in range(4):
                        acc[m * 4 + t] = acc[m * 4 + t] + factor * lanes[t]
            return tuple(acc)

        return jnp.concatenate(lax.fori_loop(0, steps, step, start, unroll=unroll), axis=0)

    zeros = tuple(jnp.zeros((8, 128), F32) for _ in range(32))

    def slab_sum(t):
        for d in NEAR:
            out.recv(block(t, (me.y + 4 - d) % 4), gy.at[t, d - 1])
        z = z_of(t)
        wide[pl.ds(pl.multiple_of(z * 512, 512), 512), :] = (
            grad_all[pl.ds(z * 4, 4)].reshape(512, 128).astype(F32)
        )
        grad = contract(
            [lambda s, m: (z * 8 + m) * 64 + s], pair_value, [lambda s: s * 32], 64, zeros, 4
        )
        slab_grad[pl.ds(pl.multiple_of(z * 256, 256), 256), :] = grad
        rounded = grad.astype(BF16)
        partial[0, z] = rounded[:128, :]
        partial[1, z] = rounded[128:, :]
        out.send(partial.at[1 - me.core, z], p_core.at[z], pc_sems.at[t], twin)

    def slab_push(t):
        z = z_of(t)
        out.recv(p_core.at[z], pc_sems.at[t])
        mine = pl.ds(pl.multiple_of(z * 256 + me.core * 128, 128), 128)
        both = slab_grad[mine, :] + p_core[z].astype(F32)
        p_wide[z] = both
        p_one[z] = both.astype(BF16)
        d = (z // 2 + 4 - me.x) % 4
        slot = (d + 3) % 4 % 3
        out.send(
            p_one.at[z], p_x.at[slot, z % 2], px_sems.at[slot, z % 2], me.at(x=z // 2), d != 0
        )

    def slab_owner(h):
        sums = p_wide[me.x * 2 + h]
        for d in NEAR:
            out.recv(p_x.at[d - 1, h], px_sems.at[d - 1, h])
            sums = sums + p_x[d - 1, h].astype(F32)
        return sums

    def slab_back(t):
        z = z_of(t)
        rows = pl.ds(pl.multiple_of(z * 256, 256), 256)
        grad = slab_grad[rows, :]
        both_s[:, :128] = (grad * slab_lin[rows, :]).astype(BF16)
        both_s[:, 128:] = (grad * slab_gate[rows, :]).astype(BF16)
        source = slab_all[pl.ds(z * 2, 2)].reshape(256, 128)
        sum_a[...] += lax.dot_general(
            source, both_s[...], (((0,), (0,)), ((), ())), preferred_element_type=F32
        )

    def pair_pass(ts, first, last, begin=0, end=8):
        zz = [z_of(t) for t in ts]

        @pl.loop(begin, end)
        def _(n):
            rows = pl.ds(pl.multiple_of(n * 256, 256), 256)
            start = zeros
            if not first:
                start = tuple(
                    pair_grad[pl.ds(pl.multiple_of(n * 256 + t * 8, 8), 8), :] for t in range(32)
                )
            grad = contract(
                [lambda s, m, z=z: (z * 8 + s) * 64 + n * 8 + m for z in zz],
                slab_value,
                [lambda s, z=z: (z * 8 + s) * 32 for z in zz],
                8,
                start,
                1 if len(ts) > 3 else (2 if len(ts) > 1 else 4),
            )
            if not last:
                pair_grad[rows, :] = grad
            else:
                both_d[rows, :128] = (grad * pair_lin[rows, :]).astype(BF16)
                both_d[rows, 128:] = (grad * pair_gate[rows, :]).astype(BF16)
                sum_b[...] += lax.dot_general(
                    pair_ref[rows, :], both_d[rows, :], (((0,), (0,)), ((), ())),
                    preferred_element_type=F32,
                )

    def slab_forward(h):
        for d in range(4):
            out.recv(slab_all.at[col_of(h, d, 1 - me.core)], sc.at[h, d])

        @pl.loop(0, 4)
        def _(n):
            forward(
                n * 2 + (me.h if h == 0 else 1 - me.h), 0, mask_slab,
                lambda n: slab_all[pl.ds(n * 2, 2)].reshape(256, 128), both_a,
                slab_value, slab_lin, slab_gate,
            )

    odd = (me.z + me.h) % 2
    for t in (1, 3, 2):
        spread(t)
    slab_round(0)
    spread(4)
    out.send(slab_own, slab_own, sh.at[0], far)
    slab_sum(0)
    slab_forward(0)
    slab_sum(1)
    slab_sum(3)
    spread(5)
    spread(7)
    spread(6)
    slab_push(0)
    slab_push(1)
    slab_sum(2)
    pair_pass((odd, 2 + odd), True, False)
    slab_push(3)
    slab_push(2)
    slab_back(odd)
    slab_back(2 + odd)
    slab_sum(4)
    spot = slab_all.at[col_of(1, 0)]
    out.recv(spot, sh.at[0])
    for d in NEAR:
        out.send(spot, spot, sx.at[1, d - 1], xs[d - 1])
    out.send(spot, spot, sc.at[1, 0], twin)
    slab_sum(5)
    slab_sum(7)
    slab_push(4)
    slab_push(5)
    slab_sum(6)
    slab_push(7)
    pair_pass((4 + odd, 6 + odd), False, False)
    slab_push(6)
    slab_round(1)
    slab_back(4 + odd)
    slab_back(6 + odd)
    slab_forward(1)
    for t in (1, 3, 5, 7):
        slab_back(t - odd)
    hand_over = out.make(weights.at[1 - me.core], w_core, c_sem.at[0], twin)
    scatter = [
        out.make(
            w_one.at[((me.x + dx) % 4) * 4 + (me.y + dy) % 4], w_xy.at[n], xy_sems.at[n], xys[n]
        )
        for n, (dx, dy) in enumerate(XY)
    ]

    def side_sums(n, acc):
        for part in range(2):
            half = acc[:, part * 128 : part * 128 + 128].reshape(8, 16, 128)
            weights[n, pl.ds(part * 8, 8)] = half
        pl.when(me.core != n)(hand_over.start)

    def side_scatter(n):
        @pl.when(me.core == n)
        def _():
            out.recv(w_core, c_sem.at[0])
            w_one[...] = weights[n] + w_core[...]
            for copy in scatter:
                copy.start()

    last = (1 - odd, 3 - odd, 5 - odd, 7 - odd)
    side_sums(0, sum_a)
    pair_pass(last, False, True, 0, 4)
    side_scatter(0)
    p_two[...] = slab_owner(1 - me.h)
    out.send(p_two, p_h, ph_sem.at[0], far)
    pair_pass(last, False, True, 4, 8)
    side_sums(1, sum_b)
    side_scatter(1)
    sums = w_one[me.x * 4 + me.y]
    for n in range(15):
        out.recv(w_xy.at[n], xy_sems.at[n])
        sums = sums + w_xy[n]
    w_two[...] = sums
    w_z[depth] = sums
    for d in (8, 7, 9, 6, 10, 5, 11, 4, 12, 3, 13, 2, 14, 1, 15):
        out.send(w_two, w_z.at[depth], z_sems.at[d - 1], zs[d - 1])


    @pl.loop(0, 8)
    def _(n):
        rows = pl.ds(pl.multiple_of(n * 256, 256), 256)
        grad_pair[rows, :] = lax.dot_general(
            both_d[rows, :], both_b[...], (((1,), (1,)), ((), ())), preferred_element_type=F32
        ).astype(BF16)

    for d in (1, 15, 2, 14, 3, 13, 4, 12, 5, 11, 6, 10, 7, 9, 8):
        out.recv(w_z.at[(depth + 16 - d) % 16], z_sems.at[d - 1])
    sums = w_z[0]
    for n in range(1, 16):
        sums = sums + w_z[n]
    place = me.x * 4 + me.y
    total[me.core, place] = sums * (1.0 / 1024.0)
    spot = total.at[me.core, place]
    for n, (dx, dy) in enumerate(XY):
        out.send(spot, spot, xyg_sems.at[n], xys[n])
    out.send(spot, spot, cg_sems.at[15], twin)

    grad = slab_owner(me.h)
    out.recv(p_h, ph_sem.at[0])
    grad = grad + p_h[...]
    rows = pl.ds(pl.multiple_of(me.col * 128, 128), 128)
    both_s[:128, :128] = (grad * slab_lin[rows, :]).astype(BF16)
    both_s[:128, 128:] = (grad * slab_gate[rows, :]).astype(BF16)
    grad_slab[...] = lax.dot_general(
        both_s[:128, :], both_a[...], (((1,), (1,)), ((), ())), preferred_element_type=F32
    ).astype(BF16)

    parts = [((me.x + 4 - dx) % 4) * 4 + (me.y + 4 - dy) % 4 for dx, dy in XY]
    for n in range(15):
        spot = total.at[me.core, parts[n]]
        out.recv(spot, xyg_sems.at[n])
        out.send(spot, spot, cg_sems.at[n], twin)
    for n in range(15):
        out.recv(total.at[1 - me.core, parts[n]], cg_sems.at[n])
    out.recv(total.at[1 - me.core, place], cg_sems.at[15])
    out.finish()


def settle_kernel(*refs):
    sources, targets, sems = refs[:3], refs[3:6], refs[6]
    stores = [pltpu.make_async_copy(sources[n], targets[n], sems.at[n]) for n in range(3)]
    for store in stores:
        store.start()
    for store in stores:
        store.wait()


OUTS = (((128, 128), BF16), ((2048, 128), BF16), ((2, 16, 16, 128), F32))
SHAPES = tuple(jax.ShapeDtypeStruct(*out) for out in OUTS)
HELD = tuple(pltpu.VMEM(*out) for out in OUTS)
VMEM = pl.BlockSpec(memory_space=pltpu.VMEM)


def settle(*arrays):
    return pl.pallas_call(
        settle_kernel,
        out_shape=SHAPES,
        in_specs=[ANY] * 3,
        out_specs=(ANY,) * 3,
        scratch_shapes=[pltpu.SemaphoreType.DMA((3,))],
        name="settle",
    )(*(pltpu.with_memory_space_constraint(a, pltpu.VMEM) for a in arrays))


def on_device(
    pair_slab, pair_full, grad_out, w_a_lin, w_a_gate, w_b_lin, w_b_gate, mask_slab, mask_residue
):
    dma = pltpu.SemaphoreType.DMA
    rows_f32 = pltpu.VMEM((2048, 128), F32)
    grad_slab, grad_pair, total = pl.pallas_call(
        whole_kernel,
        out_shape=HELD,
        in_specs=[ANY] * 9,
        out_specs=(VMEM,) * 3,
        scratch_shapes=[
            pltpu.VMEM((2048, 128), BF16),
            pltpu.SMEM((64,), jnp.int32),
            pltpu.SMEM((1024,), jnp.int32),
            dma((9,)),
            pltpu.VMEM((32, 2, 64, 128), BF16),
            pltpu.VMEM((16, 4, 32, 128), BF16),
            pltpu.VMEM((4096, 128), F32),
            pltpu.VMEM((128, 256), BF16),
            pltpu.VMEM((128, 256), BF16),
            rows_f32, rows_f32, rows_f32, rows_f32, rows_f32, rows_f32, rows_f32, rows_f32,
            pltpu.VMEM((2048, 256), BF16),
            pltpu.VMEM((256, 256), BF16),
            pltpu.VMEM((128, 256), F32),
            pltpu.VMEM((128, 256), F32),
            pltpu.VMEM((2, 8, 128, 128), BF16),
            pltpu.VMEM((8, 128, 128), BF16),
            pltpu.VMEM((8, 128, 128), F32),
            pltpu.VMEM((8, 128, 128), BF16),
            pltpu.VMEM((3, 2, 128, 128), BF16),
            pltpu.VMEM((128, 128), F32),
            pltpu.VMEM((128, 128), F32),
            pltpu.VMEM((2, 16, 16, 128), F32),
            pltpu.VMEM((16, 16, 128), F32),
            pltpu.VMEM((16, 16, 128), F32),
            pltpu.VMEM((15, 16, 128), F32),
            pltpu.VMEM((16, 128), F32),
            pltpu.VMEM((16, 16, 128), F32),
            dma((SENDS,)), dma((7,)), dma((8, 3)), dma((1,)), dma((2, 3)), dma((2, 4)),
            dma((8,)), dma((3, 2)), dma((1,)), dma((1,)), dma((15,)), dma((15,)), dma((15,)), dma((16,)),
        ],
        compiler_params=pltpu.CompilerParams(collective_id=0, has_side_effects=True),
        name="whole",
    )(
        grad_out, pair_slab, pair_full.reshape(2048, 128),
        w_a_lin, w_a_gate, w_b_lin, w_b_gate, mask_slab, mask_residue,
    )
    grad_slab, grad_pair, total = settle(grad_slab, grad_pair, total)
    return (
        grad_slab.reshape(4, 32, 128),
        grad_pair.reshape(64, 32, 128),
        total.reshape(4, 128, 128),
    )


def solution(mesh):
    return jax.shard_map(
        on_device,
        mesh=mesh,
        in_specs=(
            P("col", "row", None),
            P("col", "row", None),
            P("row", "col", None),
            P(),
            P(),
            P(),
            P(),
            P(),
            P(),
        ),
        out_specs=(P("col", "row", None), P("col", "row", None), P()),
        check_vma=False,
    )
```

```python
import jax
import jax.numpy as jnp
from jax import lax
from jax.experimental import pallas as pl
from jax.experimental.pallas import tpu as pltpu
from jax.sharding import PartitionSpec as P

MESH = pl.DeviceIdType.MESH
F32 = jnp.float32
BF16 = jnp.bfloat16
ANY = pl.BlockSpec(memory_space=pl.ANY)


class Here:
    def __init__(self):
        row = lax.axis_index("row")
        col = lax.axis_index("col")
        self.row, self.col = row, col
        self.z, self.y = row // 4, row % 4
        self.x, self.h, self.core = col // 4, (col // 2) % 2, col % 2

    def at(self, z=None, y=None, x=None, h=None, core=None):
        z = self.z if z is None else z
        y = self.y if y is None else y
        x = self.x if x is None else x
        h = self.h if h is None else h
        core = self.core if core is None else core
        return (z * 4 + y, x * 4 + h * 2 + core)


class Sender:
    def __init__(self, send_sems, anyone):
        self.send_sems, self.anyone = send_sems, anyone
        self.started = []

    def send(self, src, dst, recv_sem, device, only=None):
        copy = self.make(src, dst, recv_sem, device, only)
        if only is None:
            copy.start()
        else:
            pl.when(only)(copy.start)

    def make(self, src, dst, recv_sem, device, only=None):
        copy = pltpu.make_async_remote_copy(
            src_ref=src,
            dst_ref=dst,
            send_sem=self.send_sems.at[len(self.started)],
            recv_sem=recv_sem,
            device_id=device,
            device_id_type=MESH,
        )
        self.started.append((copy, only))
        return copy

    def recv(self, dst, recv_sem):
        pltpu.make_async_remote_copy(
            src_ref=dst,
            dst_ref=dst,
            send_sem=self.send_sems.at[0],
            recv_sem=recv_sem,
            device_id=self.anyone,
            device_id_type=MESH,
        ).wait_recv()

    def finish(self):
        for copy, only in self.started:
            if only is None:
                copy.wait_send()
            else:
                pl.when(only)(copy.wait_send)


def key_mask(mask_ref, base):
    spots = lax.broadcasted_iota(jnp.int32, (32, 128), 0)
    flags = jnp.zeros((32, 128), F32)
    for k in range(32):
        flags = jnp.where(spots == k, mask_ref[base + k].astype(F32), flags)
    return flags


def gates(rows, both, flags):
    product = jnp.dot(rows, both, preferred_element_type=F32)
    linear, sigmoid = product[:, :128], jax.nn.sigmoid(product[:, 128:])
    to_linear = flags * sigmoid
    return to_linear * linear, to_linear, to_linear * linear * (1.0 - sigmoid)


SENDS = 7 + 24 + 15 + 8 + 8 + 1 + 1 + 15 + 15 + 15 + 16
NEAR = (1, 3, 2)
XY = tuple((dx, dy) for dx in range(4) for dy in range(4))[1:]


def whole_kernel(
    grad_in, slab_in, pair_in, wal, wag, wbl, wbg, mask_slab_in, mask_res_in,
    grad_slab, grad_pair, total,
    pair_ref, mask_slab, mask_res, in_sems,
    grad_all, slab_all, wide,
    both_a, both_b, slab_value, slab_lin, slab_gate, pair_value, pair_lin, pair_gate,
    slab_grad, pair_grad, both_d, both_s, sum_a, sum_b, partial,
    p_core, p_wide, p_one, p_x, p_two, p_h,
    weights, w_core, w_one, w_xy, w_two, w_z,
    send_sems, gz, gy, sh, sx, sc, pc_sems, px_sems, ph_sem, c_sem, xy_sems, z_sems, xyg_sems, cg_sems,
):
    me = Here()
    zg, zl = me.z // 4, me.z % 4
    depth = me.h * 8 + me.z

    def deep(d):
        place = (depth + d) % 16
        return me.at(z=place % 8, h=place // 8)

    group = [me.at(z=zg * 4 + (zl + d) % 4) for d in (1, 2, 3)]
    across = me.at(z=(1 - zg) * 4 + zl)
    ys = [me.at(y=(me.y + d) % 4) for d in (1, 2, 3)]
    xs = [me.at(x=(me.x + d) % 4) for d in (1, 2, 3)]
    xys = [me.at(x=(me.x + dx) % 4, y=(me.y + dy) % 4) for dx, dy in XY]
    zs = [deep(d) for d in range(1, 16)]
    far = me.at(h=1 - me.h)
    twin = me.at(core=1 - me.core)

    peers = [twin] + xys + [deep(d) for d in (1, 2, 3, 4, 12, 13, 14, 15)]
    barrier = pltpu.get_barrier_semaphore()
    for peer in peers:
        pl.semaphore_signal(barrier, inc=1, device_id=peer, device_id_type=MESH)

    own = grad_all.at[me.row]
    slab_own = slab_all.at[me.col]
    loads = [
        pltpu.make_async_copy(source, target, in_sems.at[n])
        for n, (source, target) in enumerate(
            (
                (slab_in, slab_own),
                (grad_in, own),
                (mask_res_in, mask_res),
                (mask_slab_in, mask_slab),
                (wbl, both_b.at[:, pl.ds(0, 128)]),
                (wbg, both_b.at[:, pl.ds(128, 128)]),
                (pair_in, pair_ref),
                (wal, both_a.at[:, pl.ds(0, 128)]),
                (wag, both_a.at[:, pl.ds(128, 128)]),
            )
        )
    ]
    for load in loads:
        load.start()
    pl.semaphore_wait(barrier, len(peers))
    for load in loads[:2]:
        load.wait()
    out = Sender(send_sems, twin)

    def z_of(t):
        return (zg + t // 4) % 2 * 4 + (zl + 4 - t % 4) % 4

    def block(t, y=None):
        return grad_all.at[z_of(t) * 4 + (me.y if y is None else y)]

    def col_of(u, d, core=None):
        h = me.h if u == 0 else 1 - me.h
        return ((me.x + 4 - d) % 4) * 4 + h * 2 + (me.core if core is None else core)

    out.send(own, own, gz.at[3], across)
    for d in NEAR:
        out.send(own, own, gz.at[d - 1], group[d - 1])
    for d in NEAR:
        out.send(own, own, gy.at[0, d - 1], ys[d - 1])
    for d in NEAR:
        out.send(slab_own, slab_own, sx.at[0, d - 1], xs[d - 1])
    out.send(slab_own, slab_own, sc.at[0, 0], twin)

    for load in loads[2:]:
        load.wait()
    keys = key_mask(mask_res, me.row * 32)

    def forward(n, first, mask, rows_ref, both, value, to_lin, to_gate):
        rows = pl.ds(pl.multiple_of(n * 256, 256), 256)
        flags = jnp.concatenate(
            [keys * mask[first + n * 8 + m].astype(F32) for m in range(8)], axis=0
        )
        val, lin, gate = gates(rows_ref(n), both[...], flags)
        value[rows, :] = val.astype(BF16).astype(F32)
        to_lin[rows, :] = lin
        to_gate[rows, :] = gate

    @pl.loop(0, 8)
    def _(n):
        rows = pl.ds(pl.multiple_of(n * 256, 256), 256)
        forward(n, me.col * 64, mask_res, lambda n: pair_ref[rows, :], both_b, pair_value, pair_lin, pair_gate)

    sum_a[...] = jnp.zeros_like(sum_a)
    sum_b[...] = jnp.zeros_like(sum_b)
    def spread(t):
        out.recv(block(t), gz.at[t - 1])
        if t == 4:
            for d in (2, 1, 3):
                out.send(block(t), block(t), gz.at[3 + d], group[d - 1])
            out.send(slab_own, slab_own, sh.at[0], far)
        for d in (2, 1, 3):
            out.send(block(t), block(t), gy.at[t, d - 1], ys[d - 1])

    def slab_round(u):
        for d in NEAR:
            spot = slab_all.at[col_of(u, d)]
            out.recv(spot, sx.at[u, d - 1])
            out.send(spot, spot, sc.at[u, d], twin)

    def contract(scalar_rows, vectors, vector_row, steps, start, unroll):
        def step(s, acc):
            acc = list(acc)
            for scalar_row, base in zip(scalar_rows, vector_row):
                first = base(s)
                lanes = [vectors[pl.ds(pl.multiple_of(first + t * 8, 8), 8), :] for t in range(4)]
                for m in range(8):
                    factor = wide[pl.ds(scalar_row(s, m), 8, stride=0), :]
                    for t in range(4):
                        acc[m * 4 + t] = acc[m * 4 + t] + factor * lanes[t]
            return tuple(acc)

        return jnp.concatenate(lax.fori_loop(0, steps, step, start, unroll=unroll), axis=0)

    zeros = tuple(jnp.zeros((8, 128), F32) for _ in range(32))

    def slab_sum(t):
        for d in NEAR:
            out.recv(block(t, (me.y + 4 - d) % 4), gy.at[t, d - 1])
        z = z_of(t)
        wide[pl.ds(pl.multiple_of(z * 512, 512), 512), :] = (
            grad_all[pl.ds(z * 4, 4)].reshape(512, 128).astype(F32)
        )
        grad = contract(
            [lambda s, m: (z * 8 + m) * 64 + s], pair_value, [lambda s: s * 32], 64, zeros, 4
        )
        slab_grad[pl.ds(pl.multiple_of(z * 256, 256), 256), :] = grad
        rounded = grad.astype(BF16)
        partial[0, z] = rounded[:128, :]
        partial[1, z] = rounded[128:, :]
        out.send(partial.at[1 - me.core, z], p_core.at[z], pc_sems.at[t], twin)

    def slab_push(t):
        z = z_of(t)
        out.recv(p_core.at[z], pc_sems.at[t])
        mine = pl.ds(pl.multiple_of(z * 256 + me.core * 128, 128), 128)
        both = slab_grad[mine, :] + p_core[z].astype(F32)
        p_wide[z] = both
        p_one[z] = both.astype(BF16)
        d = (z // 2 + 4 - me.x) % 4
        slot = (d + 3) % 4 % 3
        out.send(
            p_one.at[z], p_x.at[slot, z % 2], px_sems.at[slot, z % 2], me.at(x=z // 2), d != 0
        )

    def slab_owner(h):
        sums = p_wide[me.x * 2 + h]
        for d in NEAR:
            out.recv(p_x.at[d - 1, h], px_sems.at[d - 1, h])
            sums = sums + p_x[d - 1, h].astype(F32)
        return sums

    def slab_back(t):
        z = z_of(t)
        rows = pl.ds(pl.multiple_of(z * 256, 256), 256)
        grad = slab_grad[rows, :]
        both_s[:, :128] = (grad * slab_lin[rows, :]).astype(BF16)
        both_s[:, 128:] = (grad * slab_gate[rows, :]).astype(BF16)
        source = slab_all[pl.ds(z * 2, 2)].reshape(256, 128)
        sum_a[...] += lax.dot_general(
            source, both_s[...], (((0,), (0,)), ((), ())), preferred_element_type=F32
        )

    def pair_pass(ts, first, last, begin=0, end=8):
        zz = [z_of(t) for t in ts]

        @pl.loop(begin, end)
        def _(n):
            rows = pl.ds(pl.multiple_of(n * 256, 256), 256)
            start = zeros
            if not first:
                start = tuple(
                    pair_grad[pl.ds(pl.multiple_of(n * 256 + t * 8, 8), 8), :] for t in range(32)
                )
            grad = contract(
                [lambda s, m, z=z: (z * 8 + s) * 64 + n * 8 + m for z in zz],
                slab_value,
                [lambda s, z=z: (z * 8 + s) * 32 for z in zz],
                8,
                start,
                1 if len(ts) > 3 else (2 if len(ts) > 1 else 4),
            )
            if not last:
                pair_grad[rows, :] = grad
            else:
                both_d[rows, :128] = (grad * pair_lin[rows, :]).astype(BF16)
                both_d[rows, 128:] = (grad * pair_gate[rows, :]).astype(BF16)
                sum_b[...] += lax.dot_general(
                    pair_ref[rows, :], both_d[rows, :], (((0,), (0,)), ((), ())),
                    preferred_element_type=F32,
                )

    def slab_forward(h):
        for d in range(4):
            out.recv(slab_all.at[col_of(h, d, 1 - me.core)], sc.at[h, d])

        @pl.loop(0, 4)
        def _(n):
            forward(
                n * 2 + (me.h if h == 0 else 1 - me.h), 0, mask_slab,
                lambda n: slab_all[pl.ds(n * 2, 2)].reshape(256, 128), both_a,
                slab_value, slab_lin, slab_gate,
            )

    odd = (me.z + me.h) % 2
    for t in (1, 3, 2):
        spread(t)
    spread(4)
    slab_round(0)
    slab_sum(0)
    slab_forward(0)
    slab_sum(1)
    slab_sum(3)
    spread(5)
    spread(7)
    spread(6)
    slab_push(0)
    slab_push(1)
    slab_sum(2)
    pair_pass((odd, 2 + odd), True, False)
    slab_push(3)
    slab_push(2)
    slab_back(odd)
    slab_back(2 + odd)
    slab_sum(4)
    spot = slab_all.at[col_of(1, 0)]
    out.recv(spot, sh.at[0])
    for d in NEAR:
        out.send(spot, spot, sx.at[1, d - 1], xs[d - 1])
    out.send(spot, spot, sc.at[1, 0], twin)
    slab_sum(5)
    slab_sum(7)
    slab_push(4)
    slab_push(5)
    slab_sum(6)
    slab_push(7)
    pair_pass((4 + odd, 6 + odd), False, False)
    slab_push(6)
    slab_round(1)
    slab_back(4 + odd)
    slab_back(6 + odd)
    slab_forward(1)
    for t in (1, 3, 5, 7):
        slab_back(t - odd)
    hand_over = out.make(weights.at[1 - me.core], w_core, c_sem.at[0], twin)
    scatter = [
        out.make(
            w_one.at[((me.x + dx) % 4) * 4 + (me.y + dy) % 4], w_xy.at[n], xy_sems.at[n], xys[n]
        )
        for n, (dx, dy) in enumerate(XY)
    ]

    def side_sums(n, acc):
        for part in range(2):
            half = acc[:, part * 128 : part * 128 + 128].reshape(8, 16, 128)
            weights[n, pl.ds(part * 8, 8)] = half
        pl.when(me.core != n)(hand_over.start)

    def side_scatter(n):
        @pl.when(me.core == n)
        def _():
            out.recv(w_core, c_sem.at[0])
            w_one[...] = weights[n] + w_core[...]
            for copy in scatter:
                copy.start()

    last = (1 - odd, 3 - odd, 5 - odd, 7 - odd)
    side_sums(0, sum_a)
    pair_pass(last, False, True, 0, 4)
    side_scatter(0)
    p_two[...] = slab_owner(1 - me.h)
    out.send(p_two, p_h, ph_sem.at[0], far)
    pair_pass(last, False, True, 4, 8)
    side_sums(1, sum_b)
    side_scatter(1)
    sums = w_one[me.x * 4 + me.y]
    for n in range(15):
        out.recv(w_xy.at[n], xy_sems.at[n])
        sums = sums + w_xy[n]
    w_two[...] = sums
    w_z[depth] = sums
    for d in (8, 7, 9, 6, 10, 5, 11, 4, 12, 3, 13, 2, 14, 1, 15):
        out.send(w_two, w_z.at[depth], z_sems.at[d - 1], zs[d - 1])


    @pl.loop(0, 8)
    def _(n):
        rows = pl.ds(pl.multiple_of(n * 256, 256), 256)
        grad_pair[rows, :] = lax.dot_general(
            both_d[rows, :], both_b[...], (((1,), (1,)), ((), ())), preferred_element_type=F32
        ).astype(BF16)

    for d in (1, 15, 2, 14, 3, 13, 4, 12, 5, 11, 6, 10, 7, 9, 8):
        out.recv(w_z.at[(depth + 16 - d) % 16], z_sems.at[d - 1])
    sums = w_z[0]
    for n in range(1, 16):
        sums = sums + w_z[n]
    place = me.x * 4 + me.y
    total[me.core, place] = sums * (1.0 / 1024.0)
    spot = total.at[me.core, place]
    for n, (dx, dy) in enumerate(XY):
        out.send(spot, spot, xyg_sems.at[n], xys[n])
    out.send(spot, spot, cg_sems.at[15], twin)

    grad = slab_owner(me.h)
    out.recv(p_h, ph_sem.at[0])
    grad = grad + p_h[...]
    rows = pl.ds(pl.multiple_of(me.col * 128, 128), 128)
    both_s[:128, :128] = (grad * slab_lin[rows, :]).astype(BF16)
    both_s[:128, 128:] = (grad * slab_gate[rows, :]).astype(BF16)
    grad_slab[...] = lax.dot_general(
        both_s[:128, :], both_a[...], (((1,), (1,)), ((), ())), preferred_element_type=F32
    ).astype(BF16)

    parts = [((me.x + 4 - dx) % 4) * 4 + (me.y + 4 - dy) % 4 for dx, dy in XY]
    for n in range(15):
        spot = total.at[me.core, parts[n]]
        out.recv(spot, xyg_sems.at[n])
        out.send(spot, spot, cg_sems.at[n], twin)
    for n in range(15):
        out.recv(total.at[1 - me.core, parts[n]], cg_sems.at[n])
    out.recv(total.at[1 - me.core, place], cg_sems.at[15])
    out.finish()


def settle_kernel(*refs):
    sources, targets, sems = refs[:3], refs[3:6], refs[6]
    stores = [pltpu.make_async_copy(sources[n], targets[n], sems.at[n]) for n in range(3)]
    for store in stores:
        store.start()
    for store in stores:
        store.wait()


OUTS = (((128, 128), BF16), ((2048, 128), BF16), ((2, 16, 16, 128), F32))
SHAPES = tuple(jax.ShapeDtypeStruct(*out) for out in OUTS)
HELD = tuple(pltpu.VMEM(*out) for out in OUTS)
VMEM = pl.BlockSpec(memory_space=pltpu.VMEM)


def settle(*arrays):
    return pl.pallas_call(
        settle_kernel,
        out_shape=SHAPES,
        in_specs=[ANY] * 3,
        out_specs=(ANY,) * 3,
        scratch_shapes=[pltpu.SemaphoreType.DMA((3,))],
        name="settle",
    )(*(pltpu.with_memory_space_constraint(a, pltpu.VMEM) for a in arrays))


def on_device(
    pair_slab, pair_full, grad_out, w_a_lin, w_a_gate, w_b_lin, w_b_gate, mask_slab, mask_residue
):
    dma = pltpu.SemaphoreType.DMA
    rows_f32 = pltpu.VMEM((2048, 128), F32)
    grad_slab, grad_pair, total = pl.pallas_call(
        whole_kernel,
        out_shape=HELD,
        in_specs=[ANY] * 9,
        out_specs=(VMEM,) * 3,
        scratch_shapes=[
            pltpu.VMEM((2048, 128), BF16),
            pltpu.SMEM((64,), jnp.int32),
            pltpu.SMEM((1024,), jnp.int32),
            dma((9,)),
            pltpu.VMEM((32, 2, 64, 128), BF16),
            pltpu.VMEM((16, 4, 32, 128), BF16),
            pltpu.VMEM((4096, 128), F32),
            pltpu.VMEM((128, 256), BF16),
            pltpu.VMEM((128, 256), BF16),
            rows_f32, rows_f32, rows_f32, rows_f32, rows_f32, rows_f32, rows_f32, rows_f32,
            pltpu.VMEM((2048, 256), BF16),
            pltpu.VMEM((256, 256), BF16),
            pltpu.VMEM((128, 256), F32),
            pltpu.VMEM((128, 256), F32),
            pltpu.VMEM((2, 8, 128, 128), BF16),
            pltpu.VMEM((8, 128, 128), BF16),
            pltpu.VMEM((8, 128, 128), F32),
            pltpu.VMEM((8, 128, 128), BF16),
            pltpu.VMEM((3, 2, 128, 128), BF16),
            pltpu.VMEM((128, 128), F32),
            pltpu.VMEM((128, 128), F32),
            pltpu.VMEM((2, 16, 16, 128), F32),
            pltpu.VMEM((16, 16, 128), F32),
            pltpu.VMEM((16, 16, 128), F32),
            pltpu.VMEM((15, 16, 128), F32),
            pltpu.VMEM((16, 128), F32),
            pltpu.VMEM((16, 16, 128), F32),
            dma((SENDS,)), dma((7,)), dma((8, 3)), dma((1,)), dma((2, 3)), dma((2, 4)),
            dma((8,)), dma((3, 2)), dma((1,)), dma((1,)), dma((15,)), dma((15,)), dma((15,)), dma((16,)),
        ],
        compiler_params=pltpu.CompilerParams(collective_id=0, has_side_effects=True),
        name="whole",
    )(
        grad_out, pair_slab, pair_full.reshape(2048, 128),
        w_a_lin, w_a_gate, w_b_lin, w_b_gate, mask_slab, mask_residue,
    )
    grad_slab, grad_pair, total = settle(grad_slab, grad_pair, total)
    return (
        grad_slab.reshape(4, 32, 128),
        grad_pair.reshape(64, 32, 128),
        total.reshape(4, 128, 128),
    )


def solution(mesh):
    return jax.shard_map(
        on_device,
        mesh=mesh,
        in_specs=(
            P("col", "row", None),
            P("col", "row", None),
            P("row", "col", None),
            P(),
            P(),
            P(),
            P(),
            P(),
            P(),
        ),
        out_specs=(P("col", "row", None), P("col", "row", None), P()),
        check_vma=False,
    )
```
